256 devices in a mesh: seq: 128 (over z, x, y), head: 2 (over core).
Axes of the slice: x: 4, y: 4, z: 8, core: 2. Of those that a mesh axis runs over, the one named last changes fastest.
Arguments:
- query_rows: bfloat16 [16384, 2048], P('seq', 'head'), may hold values from -6 to 6
- key_rows: bfloat16 [16384, 2048], P('seq', 'head'), may hold values from -6 to 6
- value_rows: bfloat16 [16384, 2048], P('seq', 'head'), may hold values from -6 to 6
- doc_lengths: int32 [128], replicated, may hold values from 1 to 1920, 16384 in all
- norm_gain: float32 [128], replicated, may hold values from 0.25 to 1.75
- out_weight: bfloat16 [2048, 2048], P('head'), may hold values from -0.125 to 0.125
Outputs:
- layer_out: bfloat16 [16384, 2048], P('seq', 'head')
The draws below stay inside these ranges and needn't reach their ends.
Inputs may be any that keep to these rules, and one draw needn't show every extreme that they name: `doc_lengths`: positive lengths summing to 16384; the longest has exactly 1920 tokens.
All inputs are finite; a program needn't handle non-finite values.
Results may differ from the reference program's by a relative error of at most 0.0049.
Values sent between devices are 32-bit elements; how exact they have to be, the bound alone decides.
A program may use at most 320 MiB of HBM per device.

```python
import math
import jax
import jax.numpy as jnp
import numpy as np
from jax import lax

HEADS = 16
HEAD_DIM = 128
TOK_DEV = 128
ITERS = 4
D = 2048
TOKENS = 16384
DOCS = 128
MOST = 1920


def levels(key, dims, split, smallest, top_value):
    def one(position, shards_of):
        draws = jax.random.uniform(jax.random.fold_in(jax.random.fold_in(key, 6), position), (shards_of,), jnp.float32, smallest / len(split), top_value / len(split))
        return jnp.repeat(jnp.exp(draws), dims[position] // shards_of).reshape((-1,) + (1,) * (len(dims) - position - 1))

    level = one(*split[0])
    for cut in split[1:]:
        level = level * one(*cut)
    return level


def profile(count, total, limit, lean):
    weights = [(1 << 20) // math.isqrt(standing ** lean) + 1 for standing in range(2, count + 1)]
    spare, holding = total - limit - (count - 1), [1] * (count - 1)
    while spare > 0:
        free = [i for i in range(count - 1) if holding[i] < limit]
        mass, budget = sum([weights[i] for i in free]), spare
        for i in free:
            addition = min(limit - holding[i], max(1, budget * weights[i] // mass), spare)
            holding[i] = holding[i] + addition
            spare = spare - addition
    return np.array([limit] + holding)


def ragged_sizes(stream_key, number_of, total, reach, lean):
    if number_of == 2:
        one = jax.random.randint(stream_key, (), max(1, total - reach), min(reach, total - 1) + 1)
        return jnp.stack([one, total - one])
    tallies = jnp.asarray(profile(number_of, total, reach, lean), jnp.int32)
    couples = (number_of - 1) // 2
    giver, receiver = tallies[1:1 + 2 * couples:2], tallies[2:2 + 2 * couples:2]
    room = jnp.minimum(giver - 1, reach - receiver)
    passed = jax.random.randint(jax.random.fold_in(stream_key, 1), (couples,), 0, 1 << 20) % (room + 1)
    tallies = tallies.at[1:1 + 2 * couples:2].set(giver - passed).at[2:2 + 2 * couples:2].set(receiver + passed)
    return tallies[jax.random.permutation(jax.random.fold_in(stream_key, 2), number_of)]


def normal_values(rng, extent, scale, most, split=(), kind=jnp.bfloat16):
    result = jax.random.normal(rng, extent, jnp.float32) * scale
    if len(split) > 0:
        result = levels(rng, extent, split, -0.22, 0.18) * result
    return jnp.clip(result, min=-most, max=most).astype(kind)


def setup_inputs(seed: int = 0) -> dict:
    keys = jax.random.split(jax.random.key(seed), 7)
    return {
        "query_rows": normal_values(keys[0], (TOKENS, D), 1.0, 6.0, ((0, 128), (1, 2))),
        "key_rows": normal_values(keys[1], (TOKENS, D), 1.0, 6.0, ((0, 128), (1, 2))),
        "value_rows": normal_values(keys[2], (TOKENS, D), 1.0, 6.0, ((0, 128), (1, 2))),
        "doc_lengths": ragged_sizes(keys[3], DOCS, TOKENS, MOST, 2).astype(jnp.int32),
        "norm_gain": jnp.clip(1.0 + 0.15 * jax.random.normal(keys[4], (HEAD_DIM,), jnp.float32), 0.25, 1.75),
        "out_weight": normal_values(keys[5], (D, D), D ** -0.5, 0.125, ((0, 2),)),
    }


epsilon = 1e-06
damping = 1.0
highest = lax.Precision.HIGHEST

def unit_rows(matrix_rows):
    matrix_rows = matrix_rows.astype(jnp.float32)
    return matrix_rows * lax.rsqrt(lax.optimization_barrier(jnp.sum(matrix_rows * matrix_rows, axis=-1, keepdims=True)) + epsilon)

def document_ids(doc_lengths, positions):
    starts = jnp.cumsum(doc_lengths, dtype=jnp.int32) - doc_lengths
    below = (starts[None, :] <= positions[:, None]).astype(jnp.int32)
    return lax.optimization_barrier(jnp.sum(below, axis=1, dtype=jnp.int32)) - 1

def apply_state(vector, prefix_state, carried, mask, key_block, target):
    from_prefix = jnp.einsum('htj,hij->hti', vector, prefix_state, precision=highest) * carried[None, :, None]
    scores = jnp.einsum('htj,hsj->hts', vector, key_block, precision=highest) * mask[None]
    return from_prefix + jnp.einsum('hts,hsi->hti', scores, target, precision=highest)

def solve_block(queries, key_block, value_block, gram, cross, carried, mask):
    solution = jnp.zeros_like(queries)
    residual = queries
    direction = queries
    norm_now = lax.optimization_barrier(jnp.sum(residual * residual, axis=-1, keepdims=True))
    for iteration in range(ITERS):
        product_image = apply_state(direction, gram, carried, mask, key_block, key_block) + damping * direction
        step_size = norm_now / (lax.optimization_barrier(jnp.sum(direction * product_image, axis=-1, keepdims=True)) + epsilon)
        solution = solution + step_size * direction
        residual = residual - step_size * product_image
        norm_next = lax.optimization_barrier(jnp.sum(residual * residual, axis=-1, keepdims=True))
        direction = residual + norm_next / (norm_now + epsilon) * direction
        norm_now = norm_next
    return apply_state(solution, cross, carried, mask, key_block, value_block)

def tail_states(key_block, value_block, tail_mask):
    gram = jnp.einsum('hsi,hsj->hij', key_block * tail_mask[None, :, None], key_block, precision=highest)
    cross = jnp.einsum('hsi,hsj->hij', value_block * tail_mask[None, :, None], key_block, precision=highest)
    return (gram, cross)

def reference(query_rows, key_rows, value_rows, doc_lengths, norm_gain, out_weight):
    blocks = TOKENS // TOK_DEV

    def heads_first(matrix_rows):
        return matrix_rows.reshape(blocks, TOK_DEV, HEADS, HEAD_DIM).transpose(0, 2, 1, 3)
    queries = unit_rows(heads_first(query_rows))
    keys_all = unit_rows(heads_first(key_rows))
    values = heads_first(value_rows).astype(jnp.float32)
    positions = jnp.arange(TOKENS, dtype=jnp.int32)
    doc_ids = document_ids(doc_lengths, positions).reshape(blocks, TOK_DEV)
    offsets = jnp.arange(TOK_DEV, dtype=jnp.int32)
    causal = offsets[None, :] <= offsets[:, None]

    def advance(carried_state, inputs):
        gram, cross, previous = carried_state
        query_block, key_block, value_block, block_ids = inputs
        carried = (block_ids == previous).astype(jnp.float32)
        mask = ((block_ids[:, None] == block_ids[None, :]) & causal).astype(jnp.float32)
        mixed_heads = solve_block(query_block, key_block, value_block, gram, cross, carried, mask)
        tail_mask = (block_ids == block_ids[-1]).astype(jnp.float32)
        carry_on = (block_ids[-1] == previous).astype(jnp.float32)
        tail_gram, tail_cross = tail_states(key_block, value_block, tail_mask)
        return ((tail_gram + carry_on * gram, tail_cross + carry_on * cross, block_ids[-1]), mixed_heads)
    initial = (jnp.zeros((HEADS, HEAD_DIM, HEAD_DIM), jnp.float32), jnp.zeros((HEADS, HEAD_DIM, HEAD_DIM), jnp.float32), jnp.int32(-1))
    unused, mixed_heads = lax.scan(advance, initial, (queries, keys_all, values, doc_ids))
    inverse_rms = lax.rsqrt(lax.optimization_barrier(jnp.mean(mixed_heads * mixed_heads, axis=-1, keepdims=True)) + epsilon)
    normed = (mixed_heads * inverse_rms * norm_gain).astype(jnp.bfloat16)
    normed = normed.transpose(0, 2, 1, 3).reshape(TOKENS, D)
    return jnp.dot(normed, out_weight, preferred_element_type=jnp.float32).astype(jnp.bfloat16)
```

```python
import functools

import jax
import jax.numpy as jnp
from jax import lax
from jax.experimental import pallas as pl
from jax.experimental.pallas import tpu as pltpu
from jax.sharding import PartitionSpec as P

MESH = pl.DeviceIdType.MESH
F32 = jnp.float32
BF16 = jnp.bfloat16
HD = 128
TOK = 128
HEADS = 8
PAIRS = 4
ITERS = 4
CH = 64
NB = 4
epsilon = 1e-06
damping = 1.0

WR, WZ, WC, WP, WE, WEC = 0, 4, 8, 12, 16, 32


def split2(a):
    hi = a.astype(BF16)
    return hi, (a - hi.astype(F32)).astype(BF16)


def dot(a, b, dims):
    return lax.dot_general(a, b, (dims, ((), ())), preferred_element_type=F32)


NN, NT, TN = ((1,), (0,)), ((1,), (1,)), ((0,), (0,))


def kernel(
    q_hbm, k_hbm, v_hbm, len_ref, gain_ref, w_hbm, out_ref,
    q_ref, k_ref, v_ref, w_ref,
    tbuf, ybuf, rbuf, zs, zr, eo, ebuf, xs, nbuf, acc, other,
    mask_ref, ksr, wts, tail_ref, car_ref,
    lsem, ys, yr, xsd, xr, zsd, zrv, es, er, ps, pr,
):
    s = lax.axis_index("seq")
    c = lax.axis_index("head")
    y = lax.rem(s, 4)
    row = s - y
    x = lax.rem(s // 4, 4)
    col = s - 4 * x
    z = s // 16

    def at_y(d):
        return row + lax.rem(y + d, 4)

    def at_x(d):
        return col + 4 * lax.rem(x + d, 4)

    def at_z(d):
        return lax.rem(s + 16 * d + 128, 128)

    loads = [
        pltpu.make_async_copy(k_hbm, k_ref, lsem.at[0]),
        pltpu.make_async_copy(v_hbm, v_ref, lsem.at[1]),
        pltpu.make_async_copy(q_hbm, q_ref, lsem.at[2]),
        pltpu.make_async_copy(w_hbm, w_ref, lsem.at[3]),
    ]
    for cp in loads:
        cp.start()

    barrier = pltpu.get_barrier_semaphore()
    for d in (1, 2, 3):
        pl.semaphore_signal(barrier, inc=1, device_id=(at_y(d), c), device_id_type=MESH)
        pl.semaphore_signal(barrier, inc=1, device_id=(at_x(d), c), device_id_type=MESH)
    pl.semaphore_signal(barrier, inc=1, device_id=(at_z(-1), c), device_id_type=MESH)
    pl.semaphore_signal(barrier, inc=1, device_id=(s, 1 - c), device_id_type=MESH)

    lrow = len_ref[...].astype(F32)
    ri = lax.broadcasted_iota(jnp.int32, (TOK, TOK), 0)
    ci = lax.broadcasted_iota(jnp.int32, (TOK, TOK), 1)
    lcol = jnp.sum(jnp.where(ri == ci, lrow, 0.0), axis=1, keepdims=True)
    srow = jnp.sum(jnp.where(ri < ci, lcol, 0.0), axis=0, keepdims=True)
    scol = jnp.sum(jnp.where(ci < ri, lrow, 0.0), axis=1, keepdims=True)
    base = (s * TOK).astype(F32)
    rf, cf = ri.astype(F32), ci.astype(F32)
    doc_col = jnp.sum(jnp.where(srow <= base + rf, 1.0, 0.0), axis=1, keepdims=True)
    doc_row = jnp.sum(jnp.where(scol <= base + cf, 1.0, 0.0), axis=0, keepdims=True)
    ends = jnp.sum(jnp.where(scol <= cf * TOK + (TOK - 1.0), 1.0, 0.0), axis=0, keepdims=True)
    shard = lax.broadcasted_iota(jnp.int32, (1, TOK), 1)

    def end_of(i):
        return jnp.sum(jnp.where(shard == i, ends, 0.0), axis=1, keepdims=True)

    def put(k, flag):
        wts[k : k + 1, :] = jnp.broadcast_to(jnp.where(flag, 1.0, 0.0), (1, HD))

    here, before = end_of(s), end_of(s - 1)
    car_ref[...] = jnp.broadcast_to(jnp.where(doc_col == before, 1.0, 0.0), (TOK, HD))
    tail_ref[...] = jnp.broadcast_to(jnp.where(doc_col == here, 1.0, 0.0), (TOK, HD))
    mask_ref[...] = jnp.where((doc_col == doc_row) & (ci <= ri), 1.0, 0.0)
    dy = [end_of(row + i) for i in range(4)]
    dx = [end_of(16 * z + 4 * i + 3) for i in range(4)]
    dprev, dplane = end_of(row - 1), end_of(16 * z - 1)
    for i in range(4):
        put(WR + i, dy[i] == dy[3])
        put(WZ + i, dx[i] == dx[3])
        put(WC + i, (dx[i] == dprev) & (jnp.full((1, 1), i, jnp.int32) < x))
    put(WP, (dplane == dprev) & (dplane > 0.0))
    for t in range(1, 4):
        for i in range(t):
            put(WE + 4 * t + i, dy[i] == dy[t - 1])
        put(WEC + t, dprev == dy[t - 1])

    def wt(k):
        return wts[k : k + 1, :]

    def head_cols(h):
        return pl.ds(pl.multiple_of(h * HD, HD), HD)

    def ycopy(st, d):
        return pltpu.make_async_remote_copy(
            tbuf.at[st, lax.rem(y + d, 4)], ybuf.at[st, y], ys.at[st, d - 1], yr.at[st, d - 1],
            device_id=(at_y(d), c), device_id_type=MESH,
        )

    def xcopy(st, d):
        return pltpu.make_async_remote_copy(
            rbuf.at[st, x], rbuf.at[st, x], xsd.at[st, d - 1], xr.at[st, d - 1],
            device_id=(at_x(d), c), device_id_type=MESH,
        )

    def zcopy(st):
        return pltpu.make_async_remote_copy(
            zs.at[st], zr.at[st], zsd.at[st], zrv.at[st],
            device_id=(at_z(1), c), device_id_type=MESH,
        )

    def ecopy(st, d):
        return pltpu.make_async_remote_copy(
            eo.at[st, lax.rem(y + d, 4)], ebuf.at[st, y], es.at[st, d - 1], er.at[st, d - 1],
            device_id=(at_y(d), c), device_id_type=MESH,
        )

    def send_tail(st):
        ybuf[st, y] = tbuf[st, y]
        for d in (1, 2, 3):
            ycopy(st, d).start()

    loads[0].wait()

    def gram_stage(g, carry):
        for i in range(2):
            h = 2 * g + i
            k = k_ref[:, head_cols(h)]
            kf = k.astype(F32)
            ks = lax.rsqrt(jnp.sum(kf * kf, axis=1, keepdims=True) + epsilon)
            ksr[pl.ds(h, 1), :] = jnp.sum(jnp.where(ri == ci, ks, 0.0), axis=0, keepdims=True)
            hi, lo = split2(kf * (ks * ks) * tail_ref[...])
            gram = dot(jnp.concatenate([hi, lo], 0), jnp.concatenate([k, k], 0), TN)
            tbuf[g, 2 * i] = gram[:CH]
            tbuf[g, 2 * i + 1] = gram[CH:]
        return carry

    def cross_stage(g, carry):
        for i in range(2):
            h = 2 * g + i
            k = k_ref[:, head_cols(h)]
            v = v_ref[:, head_cols(h)]
            kf = k.astype(F32)
            ks = lax.rsqrt(jnp.sum(kf * kf, axis=1, keepdims=True) + epsilon)
            hi, lo = split2(kf * ks * tail_ref[...])
            cross = dot(jnp.concatenate([hi, lo], 0), jnp.concatenate([v, v], 0), TN)
            tbuf[PAIRS + g, 2 * i] = cross[:CH]
            tbuf[PAIRS + g, 2 * i + 1] = cross[CH:]
        send_tail(PAIRS + g)
        return carry

    gram_stage(0, 0)
    pl.semaphore_wait(barrier, 8)
    send_tail(0)

    def gram_send(g, carry):
        gram_stage(g, carry)
        send_tail(g)
        return carry

    lax.fori_loop(1, PAIRS, gram_send, 0)
    loads[1].wait()
    lax.fori_loop(0, PAIRS, cross_stage, 0)

    def row_sum(st, carry):
        for d in (1, 2, 3):
            ycopy(st, d).wait_recv()
        total = ybuf[st, 3]
        for i in range(3):
            total = total + wt(WR + i) * ybuf[st, i]
        rbuf[st, x] = total
        for d in (1, 2, 3):
            xcopy(st, d).start()
        return carry

    def plane_sum(st, carry):
        for d in (1, 2, 3):
            xcopy(st, d).wait_recv()
        total = rbuf[st, 3]
        for i in range(3):
            total = total + wt(WZ + i) * rbuf[st, i]
        zs[st] = total
        zcopy(st).start()
        return carry

    def give_back(st, carry):
        zcopy(st).wait_recv()
        come = wt(WP) * zr[st]
        for i in range(3):
            come = come + wt(WC + i) * rbuf[st, i]
        eo[st, 0] = come
        parts = [ybuf[st, i] for i in range(3)]
        for t in range(1, 4):
            total = wt(WEC + t) * come
            for i in range(t):
                total = total + wt(WE + 4 * t + i) * parts[i]
            eo[st, t] = total
        ebuf[st, y] = eo[st, y]
        for d in (1, 2, 3):
            ecopy(st, d).start()
        return carry

    def solve(g, carry):
        for d in (1, 2, 3):
            ecopy(g, d).wait_recv()
        car = car_ref[...]
        car16 = car.astype(BF16)
        state = []
        for i in range(2):
            h = 2 * g + i
            q = q_ref[:, head_cols(h)].astype(F32)
            qn = q * lax.rsqrt(jnp.sum(q * q, axis=1, keepdims=True) + epsilon)
            k = k_ref[:, head_cols(h)]
            gram = jnp.concatenate([ebuf[g, 2 * i], ebuf[g, 2 * i + 1]], 0)
            ghi, glo = split2(gram)
            ksrow = ksr[pl.ds(h, 1), :]
            state.append(
                dict(
                    kk=jnp.concatenate([k, k], 1),
                    rhs=jnp.concatenate([ghi, ghi, glo, k, k], 0),
                    m=mask_ref[...] * (ksrow * ksrow),
                    x=None, r=qn, p=qn, n=jnp.sum(qn * qn, axis=1, keepdims=True),
                )
            )
        for it in range(ITERS):
            for e in state:
                p = e["p"]
                hi, lo = split2(p)
                sc = dot(jnp.concatenate([hi, lo], 1), e["kk"], NT) * e["m"]
                shi, slo = split2(sc)
                chi = hi * car16
                lhs = jnp.concatenate([chi, lo * car16, chi, shi, slo], 1)
                a = dot(lhs, e["rhs"], NN) + damping * p
                alpha = e["n"] / (jnp.sum(p * a, axis=1, keepdims=True) + epsilon)
                e["x"] = alpha * p if e["x"] is None else e["x"] + alpha * p
                if it < ITERS - 1:
                    e["r"] = e["r"] - alpha * a
                    new = jnp.sum(e["r"] * e["r"], axis=1, keepdims=True)
                    e["p"] = e["r"] + new / (e["n"] + epsilon) * p
                    e["n"] = new
        for i in range(2):
            xs[2 * g + i] = state[i]["x"]
        return carry

    def finish(g, carry):
        st = PAIRS + g
        for d in (1, 2, 3):
            ecopy(st, d).wait_recv()
        car16 = car_ref[...].astype(BF16)
        for i in range(2):
            h = 2 * g + i
            k = k_ref[:, head_cols(h)]
            v = v_ref[:, head_cols(h)]
            cross = jnp.concatenate([ebuf[st, 2 * i], ebuf[st, 2 * i + 1]], 0)
            xhi, xlo = split2(cross)
            hi, lo = split2(xs[h])
            m = mask_ref[...] * ksr[pl.ds(h, 1), :]
            sc = dot(jnp.concatenate([hi, lo], 1), jnp.concatenate([k, k], 1), NT) * m
            shi, slo = split2(sc)
            chi = hi * car16
            lhs = jnp.concatenate([chi, lo * car16, chi, shi, slo], 1)
            mixed = dot(lhs, jnp.concatenate([xhi, xhi, xlo, v, v], 0), NN)
            inv = lax.rsqrt(jnp.sum(mixed * mixed, axis=1, keepdims=True) / HD + epsilon)
            nbuf[:, head_cols(h)] = (mixed * inv * gain_ref[...]).astype(BF16)
        return carry

    lax.fori_loop(0, PAIRS, row_sum, 0)
    lax.fori_loop(0, PAIRS, plane_sum, 0)
    lax.fori_loop(0, PAIRS, give_back, 0)
    lax.fori_loop(PAIRS, 2 * PAIRS, row_sum, 0)
    lax.fori_loop(PAIRS, 2 * PAIRS, plane_sum, 0)
    lax.fori_loop(PAIRS, 2 * PAIRS, give_back, 0)
    loads[2].wait()
    lax.fori_loop(0, PAIRS, solve, 0)
    lax.fori_loop(0, PAIRS, finish, 0)

    loads[3].wait()
    half = HEADS * HD
    width = half // NB

    def pcopy(b):
        return pltpu.make_async_remote_copy(
            acc.at[b], other.at[b], ps.at[b], pr.at[b],
            device_id=(s, 1 - c), device_id_type=MESH,
        )

    normed = nbuf[...]
    for b in range(NB):
        cols = pl.ds(pl.multiple_of((1 - c) * half + b * width, width), width)
        acc[b] = dot(normed, w_ref[:, cols], NN)
        pcopy(b).start()
    for b in range(NB):
        cols = pl.ds(pl.multiple_of(c * half + b * width, width), width)
        mine = dot(normed, w_ref[:, cols], NN)
        pcopy(b).wait_recv()
        out_ref[:, b * width : (b + 1) * width] = (mine + other[b]).astype(BF16)

    def drain(st, carry):
        for d in (1, 2, 3):
            ycopy(st, d).wait_send()
            xcopy(st, d).wait_send()
            ecopy(st, d).wait_send()
        zcopy(st).wait_send()
        return carry

    lax.fori_loop(0, 2 * PAIRS, drain, 0)
    for b in range(NB):
        pcopy(b).wait_send()


def on_device(query_rows, key_rows, value_rows, doc_lengths, norm_gain, out_weight):
    half = HEADS * HD
    st = 2 * PAIRS
    dma = pltpu.SemaphoreType.DMA
    vm = pl.BlockSpec(memory_space=pltpu.VMEM)
    anywhere = pl.BlockSpec(memory_space=pl.ANY)
    return pl.pallas_call(
        kernel,
        out_shape=jax.ShapeDtypeStruct((TOK, half), BF16),
        in_specs=[anywhere, anywhere, anywhere, vm, vm, anywhere],
        out_specs=vm,
        scratch_shapes=[
            pltpu.VMEM((TOK, half), BF16),
            pltpu.VMEM((TOK, half), BF16),
            pltpu.VMEM((TOK, half), BF16),
            pltpu.VMEM((half, 2 * half), BF16),
            pltpu.VMEM((st, 4, CH, HD), F32),
            pltpu.VMEM((st, 4, CH, HD), F32),
            pltpu.VMEM((st, 4, CH, HD), F32),
            pltpu.VMEM((st, CH, HD), F32),
            pltpu.VMEM((st, CH, HD), F32),
            pltpu.VMEM((st, 4, CH, HD), F32),
            pltpu.VMEM((st, 4, CH, HD), F32),
            pltpu.VMEM((HEADS, TOK, HD), F32),
            pltpu.VMEM((TOK, half), BF16),
            pltpu.VMEM((NB, TOK, half // NB), F32),
            pltpu.VMEM((NB, TOK, half // NB), F32),
            pltpu.VMEM((TOK, TOK), F32),
            pltpu.VMEM((HEADS, HD), F32),
            pltpu.VMEM((40, HD), F32),
            pltpu.VMEM((TOK, HD), F32),
            pltpu.VMEM((TOK, HD), F32),
            dma((4,)),
            dma((st, 3)), dma((st, 3)),
            dma((st, 3)), dma((st, 3)),
            dma((st,)), dma((st,)),
            dma((st, 3)), dma((st, 3)),
            dma((NB,)), dma((NB,)),
        ],
        compiler_params=pltpu.CompilerParams(collective_id=0, has_side_effects=True),
        name="mesa",
    )(
        query_rows, key_rows, value_rows,
        doc_lengths.reshape(1, -1), norm_gain.reshape(1, -1), out_weight,
    )


def solution(mesh):
    in_specs = (P("seq", "head"), P("seq", "head"), P("seq", "head"), P(), P(), P("head", None))
    return jax.shard_map(
        on_device, mesh=mesh, in_specs=in_specs, out_specs=P("seq", "head"), check_vma=False
    )
```

```python
import functools

import jax
import jax.numpy as jnp
from jax import lax
from jax.experimental import pallas as pl
from jax.experimental.pallas import tpu as pltpu
from jax.sharding import PartitionSpec as P

MESH = pl.DeviceIdType.MESH
F32 = jnp.float32
BF16 = jnp.bfloat16
HD = 128
TOK = 128
HEADS = 8
PAIRS = 4
ITERS = 4
CH = 64
CG = 40
LAST = 7
NB = 4
epsilon = 1e-06
damping = 1.0

WR, WZ, WC, WP, WE, WEC = 0, 4, 8, 12, 16, 32


def split2(a):
    hi = a.astype(BF16)
    return hi, (a - hi.astype(F32)).astype(BF16)


def dot(a, b, dims):
    return lax.dot_general(a, b, (dims, ((), ())), preferred_element_type=F32)


NN, NT, TN = ((1,), (0,)), ((1,), (1,)), ((0,), (0,))


def kernel(
    q_hbm, k_hbm, v_hbm, len_ref, gain_ref, w_hbm, out_ref,
    q_ref, k_ref, v_ref, w_ref,
    tbuf, ybuf, rbuf, zs, zr, eo, ebuf, xs, nbuf, acc, other,
    mask_ref, ksr, wts, tail_ref, car_ref,
    lsem, ys, yr, xsd, xr, zsd, zrv, es, er, ps, pr, ready,
):
    s = lax.axis_index("seq")
    c = lax.axis_index("head")
    y = lax.rem(s, 4)
    row = s - y
    x = lax.rem(s // 4, 4)
    col = s - 4 * x
    z = s // 16

    def at_y(d):
        return row + lax.rem(y + d, 4)

    def at_x(d):
        return col + 4 * lax.rem(x + d, 4)

    loads = [
        pltpu.make_async_copy(k_hbm, k_ref, lsem.at[0]),
        pltpu.make_async_copy(v_hbm, v_ref, lsem.at[1]),
        pltpu.make_async_copy(q_hbm, q_ref, lsem.at[2]),
        pltpu.make_async_copy(w_hbm, w_ref, lsem.at[3]),
    ]
    barrier = pltpu.get_barrier_semaphore()
    for d in (1, 2, 3):
        pl.semaphore_signal(barrier, inc=1, device_id=(at_y(d), c), device_id_type=MESH)
        pl.semaphore_signal(barrier, inc=1, device_id=(at_x(d), c), device_id_type=MESH)
    pl.semaphore_signal(barrier, inc=1, device_id=(s, 1 - c), device_id_type=MESH)

    @pl.when(z < LAST)
    def _():
        pl.semaphore_signal(barrier, inc=1, device_id=(s + 16, c), device_id_type=MESH)

    for cp in loads:
        cp.start()

    @pl.when(z == 0)
    def _():
        zr[...] = jnp.zeros_like(zr)

    lrow = len_ref[...].astype(F32)
    ri = lax.broadcasted_iota(jnp.int32, (TOK, TOK), 0)
    ci = lax.broadcasted_iota(jnp.int32, (TOK, TOK), 1)
    lcol = jnp.sum(jnp.where(ri == ci, lrow, 0.0), axis=1, keepdims=True)
    srow = jnp.sum(jnp.where(ri < ci, lcol, 0.0), axis=0, keepdims=True)
    scol = jnp.sum(jnp.where(ci < ri, lrow, 0.0), axis=1, keepdims=True)
    base = (s * TOK).astype(F32)
    rf, cf = ri.astype(F32), ci.astype(F32)
    doc_col = jnp.sum(jnp.where(srow <= base + rf, 1.0, 0.0), axis=1, keepdims=True)
    doc_row = jnp.sum(jnp.where(scol <= base + cf, 1.0, 0.0), axis=0, keepdims=True)
    ends = jnp.sum(jnp.where(scol <= cf * TOK + (TOK - 1.0), 1.0, 0.0), axis=0, keepdims=True)
    shard = lax.broadcasted_iota(jnp.int32, (1, TOK), 1)

    def end_of(i):
        return jnp.sum(jnp.where(shard == i, ends, 0.0), axis=1, keepdims=True)

    def put(k, flag):
        wts[k : k + 1, :] = jnp.broadcast_to(jnp.where(flag, 1.0, 0.0), (1, HD))

    here, before = end_of(s), end_of(s - 1)
    car_ref[...] = jnp.broadcast_to(jnp.where(doc_col == before, 1.0, 0.0), (TOK, HD))
    tail_ref[...] = jnp.broadcast_to(jnp.where(doc_col == here, 1.0, 0.0), (TOK, HD))
    mask_ref[...] = jnp.where((doc_col == doc_row) & (ci <= ri), 1.0, 0.0)
    dy = [end_of(row + i) for i in range(4)]
    dx = [end_of(16 * z + 4 * i + 3) for i in range(4)]
    dprev, dplane = end_of(row - 1), end_of(16 * z - 1)
    for i in range(4):
        put(WR + i, dy[i] == dy[3])
        put(WZ + i, dx[i] == dx[3])
        put(WC + i, (dx[i] == dprev) & (jnp.full((1, 1), i, jnp.int32) < x))
    put(WP, (dplane == dprev) & (dplane > 0.0))
    for t in range(1, 4):
        for i in range(t):
            put(WE + 4 * t + i, dy[i] == dy[t - 1])
        put(WEC + t, dprev == dy[t - 1])

    def wt(k):
        return wts[k : k + 1, :]

    def head_cols(h):
        return pl.ds(pl.multiple_of(h * HD, HD), HD)

    def rows(st):
        return pl.ds(0, CG if st < PAIRS else CH)

    def ycopy(st, d):
        r = rows(st)
        return pltpu.make_async_remote_copy(
            tbuf.at[st, lax.rem(y + d, 4), r], ybuf.at[st, y, r],
            ys.at[st, d - 1], yr.at[st, d - 1],
            device_id=(at_y(d), c), device_id_type=MESH,
        )

    def xcopy(st, d):
        r = rows(st)
        return pltpu.make_async_remote_copy(
            rbuf.at[st, x, r], rbuf.at[st, x, r], xsd.at[st, d - 1], xr.at[st, d - 1],
            device_id=(at_x(d), c), device_id_type=MESH,
        )

    def zcopy(st):
        r = rows(st)
        return pltpu.make_async_remote_copy(
            zs.at[st, r], zr.at[st, r], zsd.at[st], zrv.at[st],
            device_id=(lax.rem(s + 16, 128), c), device_id_type=MESH,
        )

    def ecopy(st, d):
        r = rows(st)
        return pltpu.make_async_remote_copy(
            eo.at[st, lax.rem(y + d, 4), r], ebuf.at[st, y, r],
            es.at[st, d - 1], er.at[st, d - 1],
            device_id=(at_y(d), c), device_id_type=MESH,
        )

    def send_tail(st):
        r = rows(st)
        for d in (1, 2, 3):
            ycopy(st, d).start()
        ybuf[st, y, r] = tbuf[st, y, r]

    lane = lax.broadcasted_iota(jnp.int32, (32, HD), 1)

    def gram_stage(g):
        grams = []
        for h in (2 * g, 2 * g + 1):
            k = k_ref[:, head_cols(h)]
            kf = k.astype(F32)
            ks = lax.rsqrt(jnp.sum(kf * kf, axis=1, keepdims=True) + epsilon)
            ksr[h : h + 1, :] = jnp.sum(jnp.where(ri == ci, ks, 0.0), axis=0, keepdims=True)
            hi, lo = split2(kf * (ks * ks) * tail_ref[...])
            grams.append(dot(jnp.concatenate([hi, lo], 0), jnp.concatenate([k, k], 0), TN))
        blocks = []
        for gram in grams:
            blocks.append(gram[:32])
            blocks.append(jnp.where(lane < 32, pltpu.roll(gram[96:], 32, 1), gram[32:64]))
        blocks.append(jnp.where(lane < 64, pltpu.roll(grams[1][64:96], 64, 1), grams[0][64:96]))
        packed = jnp.concatenate(blocks, 0)
        for o in range(4):
            tbuf[g, o, :CG] = packed[CG * o : CG * (o + 1)]

    def gram_of(g, i):
        packed = jnp.concatenate([ebuf[g, o, :CG] for o in range(4)], 0)
        first, second, third = packed[64 * i : 64 * i + 32], packed[64 * i + 32 : 64 * i + 64], packed[128:]
        if i == 1:
            third = pltpu.roll(third, 64, 1)
        upper = jnp.concatenate([first, second, third, pltpu.roll(second, 96, 1)], 0)
        return jnp.where(ci // 32 >= ri // 32, upper, upper.T)

    def cross_stage(g):
        for i in range(2):
            h = 2 * g + i
            k = k_ref[:, head_cols(h)]
            v = v_ref[:, head_cols(h)]
            kf = k.astype(F32)
            ks = lax.rsqrt(jnp.sum(kf * kf, axis=1, keepdims=True) + epsilon)
            hi, lo = split2(kf * ks * tail_ref[...])
            cross = dot(jnp.concatenate([hi, lo], 0), jnp.concatenate([v, v], 0), TN)
            tbuf[PAIRS + g, 2 * i] = cross[:CH]
            tbuf[PAIRS + g, 2 * i + 1] = cross[CH:]

    def row_sum(st):
        r = rows(st)
        for d in (1, 2, 3):
            ycopy(st, d).wait_recv()
        total = ybuf[st, 3, r]
        for i in range(3):
            total = total + wt(WR + i) * ybuf[st, i, r]
        rbuf[st, x, r] = total
        for d in (1, 2, 3):
            xcopy(st, d).start()

    def plane_sum(st):
        r = rows(st)
        for d in (1, 2, 3):
            xcopy(st, d).wait_recv()
        total = rbuf[st, 3, r]
        for i in range(3):
            total = total + wt(WZ + i) * rbuf[st, i, r]
        zs[st, r] = total

        @pl.when(z < LAST)
        def _():
            if st == 0:
                pl.semaphore_wait(ready, 1)
            zcopy(st).start()

    def give_back(st):
        r = rows(st)

        @pl.when(z > 0)
        def _():
            zcopy(st).wait_recv()

        come = wt(WP) * zr[st, r]
        for i in range(3):
            come = come + wt(WC + i) * rbuf[st, i, r]
        eo[st, 0, r] = come
        parts = [ybuf[st, i, r] for i in range(3)]
        for t in range(1, 4):
            total = wt(WEC + t) * come
            for i in range(t):
                total = total + wt(WE + 4 * t + i) * parts[i]
            eo[st, t, r] = total
        for d in (1, 2, 3):
            ecopy(st, d).start()
        ebuf[st, y, r] = eo[st, y, r]

    def solve(g):
        for d in (1, 2, 3):
            ecopy(g, d).wait_recv()
        car = car_ref[...]
        car16 = car.astype(BF16)
        state = []
        for i in range(2):
            h = 2 * g + i
            q = q_ref[:, head_cols(h)].astype(F32)
            qn = q * lax.rsqrt(jnp.sum(q * q, axis=1, keepdims=True) + epsilon)
            k = k_ref[:, head_cols(h)]
            ghi, glo = split2(gram_of(g, i))
            ksrow = ksr[h : h + 1, :]
            state.append(
                dict(
                    kk=jnp.concatenate([k, k], 1),
                    rhs=jnp.concatenate([ghi, ghi, glo, k, k], 0),
                    m=mask_ref[...] * (ksrow * ksrow),
                    x=None, r=qn, p=qn, n=jnp.sum(qn * qn, axis=1, keepdims=True),
                )
            )
        for it in range(ITERS):
            for e in state:
                p = e["p"]
                hi, lo = split2(p)
                sc = dot(jnp.concatenate([hi, lo], 1), e["kk"], NT) * e["m"]
                shi, slo = split2(sc)
                chi = hi * car16
                lhs = jnp.concatenate([chi, lo * car16, chi, shi, slo], 1)
                a = dot(lhs, e["rhs"], NN) + damping * p
                alpha = e["n"] / (jnp.sum(p * a, axis=1, keepdims=True) + epsilon)
                e["x"] = alpha * p if e["x"] is None else e["x"] + alpha * p
                if it < ITERS - 1:
                    e["r"] = e["r"] - alpha * a
                    new = jnp.sum(e["r"] * e["r"], axis=1, keepdims=True)
                    e["p"] = e["r"] + new / (e["n"] + epsilon) * p
                    e["n"] = new
        for i in range(2):
            xs[2 * g + i] = state[i]["x"]

    def finish(g):
        st = PAIRS + g
        for d in (1, 2, 3):
            ecopy(st, d).wait_recv()
        car16 = car_ref[...].astype(BF16)
        for i in range(2):
            h = 2 * g + i
            k = k_ref[:, head_cols(h)]
            v = v_ref[:, head_cols(h)]
            cross = jnp.concatenate([ebuf[st, 2 * i], ebuf[st, 2 * i + 1]], 0)
            xhi, xlo = split2(cross)
            hi, lo = split2(xs[h])
            m = mask_ref[...] * ksr[h : h + 1, :]
            sc = dot(jnp.concatenate([hi, lo], 1), jnp.concatenate([k, k], 1), NT) * m
            shi, slo = split2(sc)
            chi = hi * car16
            lhs = jnp.concatenate([chi, lo * car16, chi, shi, slo], 1)
            mixed = dot(lhs, jnp.concatenate([xhi, xhi, xlo, v, v], 0), NN)
            inv = lax.rsqrt(jnp.sum(mixed * mixed, axis=1, keepdims=True) / HD + epsilon)
            nbuf[:, head_cols(h)] = (mixed * inv * gain_ref[...]).astype(BF16)

    loads[0].wait()
    gram_stage(0)
    pl.semaphore_wait(barrier, 7 + jnp.minimum(z, 1))

    @pl.when(z > 0)
    def _():
        pl.semaphore_signal(ready, inc=1, device_id=(s - 16, c), device_id_type=MESH)

    send_tail(0)
    for g in range(1, PAIRS):
        gram_stage(g)
        send_tail(g)
    loads[1].wait()
    for g in range(PAIRS):
        cross_stage(g)
        send_tail(PAIRS + g)
    for t in range(2 * PAIRS):
        row_sum(t)
        if t >= 2:
            plane_sum(t - 2)
        if t >= 4:
            give_back(t - 4)
    loads[2].wait()
    plane_sum(6)
    give_back(4)
    solve(0)
    plane_sum(7)
    give_back(5)
    solve(1)
    give_back(6)
    give_back(7)
    solve(2)
    solve(3)
    for g in range(PAIRS):
        finish(g)

    loads[3].wait()
    half = HEADS * HD
    width = half // NB

    def pcopy(b):
        return pltpu.make_async_remote_copy(
            acc.at[b], other.at[b], ps.at[b], pr.at[b],
            device_id=(s, 1 - c), device_id_type=MESH,
        )

    normed = nbuf[...]
    for b in range(NB):
        cols = pl.ds(pl.multiple_of((1 - c) * half + b * width, width), width)
        acc[b] = dot(normed, w_ref[:, cols], NN)
        pcopy(b).start()
    for b in range(NB):
        cols = pl.ds(pl.multiple_of(c * half + b * width, width), width)
        mine = dot(normed, w_ref[:, cols], NN)
        pcopy(b).wait_recv()
        out_ref[:, b * width : (b + 1) * width] = (mine + other[b]).astype(BF16)

    for st in range(2 * PAIRS):
        for d in (1, 2, 3):
            ycopy(st, d).wait_send()
            xcopy(st, d).wait_send()
            ecopy(st, d).wait_send()

    @pl.when(z < LAST)
    def _():
        for st in range(2 * PAIRS):
            zcopy(st).wait_send()

    for b in range(NB):
        pcopy(b).wait_send()


def on_device(query_rows, key_rows, value_rows, doc_lengths, norm_gain, out_weight):
    half = HEADS * HD
    st = 2 * PAIRS
    dma = pltpu.SemaphoreType.DMA
    vm = pl.BlockSpec(memory_space=pltpu.VMEM)
    anywhere = pl.BlockSpec(memory_space=pl.ANY)
    return pl.pallas_call(
        kernel,
        out_shape=jax.ShapeDtypeStruct((TOK, half), BF16),
        in_specs=[anywhere, anywhere, anywhere, vm, vm, anywhere],
        out_specs=vm,
        scratch_shapes=[
            pltpu.VMEM((TOK, half), BF16),
            pltpu.VMEM((TOK, half), BF16),
            pltpu.VMEM((TOK, half), BF16),
            pltpu.VMEM((half, 2 * half), BF16),
            pltpu.VMEM((st, 4, CH, HD), F32),
            pltpu.VMEM((st, 4, CH, HD), F32),
            pltpu.VMEM((st, 4, CH, HD), F32),
            pltpu.VMEM((st, CH, HD), F32),
            pltpu.VMEM((st, CH, HD), F32),
            pltpu.VMEM((st, 4, CH, HD), F32),
            pltpu.VMEM((st, 4, CH, HD), F32),
            pltpu.VMEM((HEADS, TOK, HD), F32),
            pltpu.VMEM((TOK, half), BF16),
            pltpu.VMEM((NB, TOK, half // NB), F32),
            pltpu.VMEM((NB, TOK, half // NB), F32),
            pltpu.VMEM((TOK, TOK), F32),
            pltpu.VMEM((HEADS, HD), F32),
            pltpu.VMEM((40, HD), F32),
            pltpu.VMEM((TOK, HD), F32),
            pltpu.VMEM((TOK, HD), F32),
            dma((4,)),
            dma((st, 3)), dma((st, 3)),
            dma((st, 3)), dma((st, 3)),
            dma((st,)), dma((st,)),
            dma((st, 3)), dma((st, 3)),
            dma((NB,)), dma((NB,)),
            pltpu.SemaphoreType.REGULAR,
        ],
        compiler_params=pltpu.CompilerParams(collective_id=0, has_side_effects=True),
        name="mesa",
    )(
        query_rows, key_rows, value_rows,
        doc_lengths.reshape(1, -1), norm_gain.reshape(1, -1), out_weight,
    )


def solution(mesh):
    in_specs = (P("seq", "head"), P("seq", "head"), P("seq", "head"), P(), P(), P("head", None))
    return jax.shard_map(
        on_device, mesh=mesh, in_specs=in_specs, out_specs=P("seq", "head"), check_vma=False
    )
```

```python
import jax
import jax.numpy as jnp
from jax import lax
from jax.experimental import pallas as pl
from jax.experimental.pallas import tpu as pltpu
from jax.sharding import PartitionSpec as P

MESH = pl.DeviceIdType.MESH
F32 = jnp.float32
BF16 = jnp.bfloat16
HD = 128
TOK = 128
HEADS = 8
PAIRS = 4
ITERS = 4
CH = 64
CG = 40
LAST = 7
NB = 4
epsilon = 1e-06
damping = 1.0

WR, WZ, WC, WP, WE, WEC = 0, 4, 8, 12, 16, 32


def split2(a):
    hi = a.astype(BF16)
    return hi, (a - hi.astype(F32)).astype(BF16)


def dot(a, b, dims):
    return lax.dot_general(a, b, (dims, ((), ())), preferred_element_type=F32)


NN, NT, TN = ((1,), (0,)), ((1,), (1,)), ((0,), (0,))


def kernel(
    q_hbm, k_hbm, v_hbm, len_hbm, gain_hbm, w_hbm, out_ref,
    q_ref, k_ref, v_ref, w_ref, len_ref, gain_ref,
    tbuf, ybuf, rbuf, zs, zr, eo, ebuf, qs, scq, rhs, xl, nbuf, acc, other,
    mask_ref, ksr, wts, tail_ref, car_ref,
    lsem, ys, yr, xsd, xr, zsd, zrv, es, er, ps, pr, ready,
):
    s = lax.axis_index("seq")
    c = lax.axis_index("head")
    y = lax.rem(s, 4)
    row = s - y
    x = lax.rem(s // 4, 4)
    col = s - 4 * x
    z = s // 16

    def at_y(d):
        return row + lax.rem(y + d, 4)

    def at_x(d):
        return col + 4 * lax.rem(x + d, 4)

    barrier = pltpu.get_barrier_semaphore()
    for d in (1, 2, 3):
        pl.semaphore_signal(barrier, inc=1, device_id=(at_y(d), c), device_id_type=MESH)
        pl.semaphore_signal(barrier, inc=1, device_id=(at_x(d), c), device_id_type=MESH)
    pl.semaphore_signal(barrier, inc=1, device_id=(s, 1 - c), device_id_type=MESH)

    @pl.when(z < LAST)
    def _():
        pl.semaphore_signal(barrier, inc=1, device_id=(s + 16, c), device_id_type=MESH)

    loads = [
        pltpu.make_async_copy(a, b, lsem.at[i])
        for i, (a, b) in enumerate(
            [
                (len_hbm, len_ref), (k_hbm, k_ref), (v_hbm, v_ref),
                (q_hbm, q_ref), (gain_hbm, gain_ref), (w_hbm, w_ref),
            ]
        )
    ]
    LEN, KEY, VAL, QUERY, GAIN, WEIGHT = loads
    for cp in loads:
        cp.start()

    @pl.when(z == 0)
    def _():
        zr[...] = jnp.zeros_like(zr)

    LEN.wait()
    lrow = len_ref[...].astype(F32)
    ri = lax.broadcasted_iota(jnp.int32, (TOK, TOK), 0)
    ci = lax.broadcasted_iota(jnp.int32, (TOK, TOK), 1)
    lcol = jnp.sum(jnp.where(ri == ci, lrow, 0.0), axis=1, keepdims=True)
    srow = jnp.sum(jnp.where(ri < ci, lcol, 0.0), axis=0, keepdims=True)
    scol = jnp.sum(jnp.where(ci < ri, lrow, 0.0), axis=1, keepdims=True)
    base = (s * TOK).astype(F32)
    rf, cf = ri.astype(F32), ci.astype(F32)
    doc_col = jnp.sum(jnp.where(srow <= base + rf, 1.0, 0.0), axis=1, keepdims=True)
    doc_row = jnp.sum(jnp.where(scol <= base + cf, 1.0, 0.0), axis=0, keepdims=True)
    ends = jnp.sum(jnp.where(scol <= cf * TOK + (TOK - 1.0), 1.0, 0.0), axis=0, keepdims=True)
    shard = lax.broadcasted_iota(jnp.int32, (1, TOK), 1)

    def end_of(i):
        return jnp.sum(jnp.where(shard == i, ends, 0.0), axis=1, keepdims=True)

    def put(k, flag):
        wts[k : k + 1, :] = jnp.broadcast_to(jnp.where(flag, 1.0, 0.0), (1, HD))

    here, before = end_of(s), end_of(s - 1)
    car_ref[...] = jnp.broadcast_to(jnp.where(doc_col == before, 1.0, 0.0), (TOK, HD))
    tail_ref[...] = jnp.broadcast_to(jnp.where(doc_col == here, 1.0, 0.0), (TOK, HD))
    mask_ref[...] = jnp.where((doc_col == doc_row) & (ci <= ri), 1.0, 0.0)
    dy = [end_of(row + i) for i in range(4)]
    dx = [end_of(16 * z + 4 * i + 3) for i in range(4)]
    dprev, dplane = end_of(row - 1), end_of(16 * z - 1)
    for i in range(4):
        put(WR + i, dy[i] == dy[3])
        put(WZ + i, dx[i] == dx[3])
        put(WC + i, (dx[i] == dprev) & (jnp.full((1, 1), i, jnp.int32) < x))
    put(WP, (dplane == dprev) & (dplane > 0.0))
    for t in range(1, 4):
        for i in range(t):
            put(WE + 4 * t + i, dy[i] == dy[t - 1])
        put(WEC + t, dprev == dy[t - 1])

    def wt(k):
        return wts[k : k + 1, :]

    def head_cols(h):
        return pl.ds(pl.multiple_of(h * HD, HD), HD)

    def rows(st):
        return pl.ds(0, CG if st < PAIRS else CH)

    def ycopy(st, d):
        r = rows(st)
        return pltpu.make_async_remote_copy(
            tbuf.at[st, lax.rem(y + d, 4), r], ybuf.at[st, y, r],
            ys.at[st, d - 1], yr.at[st, d - 1],
            device_id=(at_y(d), c), device_id_type=MESH,
        )

    def xcopy(st, d):
        r = rows(st)
        return pltpu.make_async_remote_copy(
            rbuf.at[st, x, r], rbuf.at[st, x, r], xsd.at[st, d - 1], xr.at[st, d - 1],
            device_id=(at_x(d), c), device_id_type=MESH,
        )

    def zcopy(st):
        r = rows(st)
        return pltpu.make_async_remote_copy(
            zs.at[st, r], zr.at[st, r], zsd.at[st], zrv.at[st],
            device_id=(lax.rem(s + 16, 128), c), device_id_type=MESH,
        )

    def ecopy(st, d):
        r = rows(st)
        return pltpu.make_async_remote_copy(
            eo.at[st, lax.rem(y + d, 4), r], ebuf.at[st, y, r],
            es.at[st, d - 1], er.at[st, d - 1],
            device_id=(at_y(d), c), device_id_type=MESH,
        )

    def send_tail(st):
        r = rows(st)
        for d in (1, 2, 3):
            ycopy(st, d).start()
        ybuf[st, y, r] = tbuf[st, y, r]

    lane = lax.broadcasted_iota(jnp.int32, (32, HD), 1)

    def gram_stage(g):
        grams = []
        for h in (2 * g, 2 * g + 1):
            k = k_ref[:, head_cols(h)]
            kf = k.astype(F32)
            ks = lax.rsqrt(jnp.sum(kf * kf, axis=1, keepdims=True) + epsilon)
            ksr[h : h + 1, :] = jnp.sum(jnp.where(ri == ci, ks, 0.0), axis=0, keepdims=True)
            hi, lo = split2(kf * (ks * ks) * tail_ref[...])
            grams.append(dot(jnp.concatenate([hi, lo], 0), jnp.concatenate([k, k], 0), TN))
        blocks = []
        for gram in grams:
            blocks.append(gram[:32])
            blocks.append(jnp.where(lane < 32, pltpu.roll(gram[96:], 32, 1), gram[32:64]))
        blocks.append(jnp.where(lane < 64, pltpu.roll(grams[1][64:96], 64, 1), grams[0][64:96]))
        packed = jnp.concatenate(blocks, 0)
        for o in range(4):
            tbuf[g, o, :CG] = packed[CG * o : CG * (o + 1)]

    def gram_of(g, i):
        packed = jnp.concatenate([ebuf[g, o, :CG] for o in range(4)], 0)
        first, second, third = packed[64 * i : 64 * i + 32], packed[64 * i + 32 : 64 * i + 64], packed[128:]
        if i == 1:
            third = pltpu.roll(third, 64, 1)
        upper = jnp.concatenate([first, second, third, pltpu.roll(second, 96, 1)], 0)
        return jnp.where(ci // 32 >= ri // 32, upper, upper.T)

    def cross_stage(g):
        for i in range(2):
            h = 2 * g + i
            k = k_ref[:, head_cols(h)]
            v = v_ref[:, head_cols(h)]
            kf = k.astype(F32)
            ks = lax.rsqrt(jnp.sum(kf * kf, axis=1, keepdims=True) + epsilon)
            hi, lo = split2(kf * ks * tail_ref[...])
            cross = dot(jnp.concatenate([hi, lo], 0), jnp.concatenate([v, v], 0), TN)
            tbuf[PAIRS + g, 2 * i] = cross[:CH]
            tbuf[PAIRS + g, 2 * i + 1] = cross[CH:]

    def row_sum(st):
        r = rows(st)
        for d in (1, 2, 3):
            ycopy(st, d).wait_recv()
        total = ybuf[st, 3, r]
        for i in range(3):
            total = total + wt(WR + i) * ybuf[st, i, r]
        rbuf[st, x, r] = total
        for d in (1, 2, 3):
            xcopy(st, d).start()

    def plane_sum(st):
        r = rows(st)
        for d in (1, 2, 3):
            xcopy(st, d).wait_recv()
        total = rbuf[st, 3, r]
        for i in range(3):
            total = total + wt(WZ + i) * rbuf[st, i, r]
        zs[st, r] = total

        @pl.when(z < LAST)
        def _():
            if st == 0:
                pl.semaphore_wait(ready, 1)
            zcopy(st).start()

    def give_back(st):
        r = rows(st)

        @pl.when(z > 0)
        def _():
            zcopy(st).wait_recv()

        come = wt(WP) * zr[st, r]
        for i in range(3):
            come = come + wt(WC + i) * rbuf[st, i, r]
        eo[st, 0, r] = come
        parts = [ybuf[st, i, r] for i in range(3)]
        for t in range(1, 4):
            total = wt(WEC + t) * come
            for i in range(t):
                total = total + wt(WE + 4 * t + i) * parts[i]
            eo[st, t, r] = total
        for d in (1, 2, 3):
            ecopy(st, d).start()
        ebuf[st, y, r] = eo[st, y, r]

    def prepare(g):
        for h in (2 * g, 2 * g + 1):
            q = q_ref[:, head_cols(h)].astype(F32)
            qn = q * lax.rsqrt(jnp.sum(q * q, axis=1, keepdims=True) + epsilon)
            k = k_ref[:, head_cols(h)]
            hi, lo = split2(qn)
            qs[h] = qn
            scq[h] = dot(jnp.concatenate([hi, lo], 1), jnp.concatenate([k, k], 1), NT)
            khi, klo = split2(dot(k, k, NT))
            both = jnp.concatenate([k, khi], 1)
            rhs[h, 3 * HD : 4 * HD] = both
            rhs[h, 4 * HD : 5 * HD] = both
            rhs[h, 5 * HD :] = jnp.concatenate([jnp.zeros_like(klo), klo], 1)

    def solve(g):
        for d in (1, 2, 3):
            ecopy(g, d).wait_recv()
        car16 = car_ref[...].astype(BF16)
        state = []
        for i in range(2):
            h = 2 * g + i
            k = k_ref[:, head_cols(h)]
            ghi, glo = split2(gram_of(g, i))
            shi, slo = split2(dot(jnp.concatenate([ghi, glo], 1), jnp.concatenate([k, k], 1), NT))
            both = jnp.concatenate([ghi, shi], 1)
            rhs[h, :HD] = both
            rhs[h, HD : 2 * HD] = both
            rhs[h, 2 * HD : 3 * HD] = jnp.concatenate([glo, slo], 1)
            ksrow = ksr[h : h + 1, :]
            qn, sc = qs[h], scq[h]
            state.append(
                dict(
                    h=h, m=mask_ref[...] * (ksrow * ksrow), p=qn, sp=sc, r=qn, sr=sc,
                    n=jnp.sum(qn * qn, axis=1, keepdims=True),
                )
            )
        for it in range(ITERS):
            last = it == ITERS - 1
            for e in state:
                p, sp = e["p"], e["sp"]
                hi, lo = split2(p)
                shi, slo = split2(sp * e["m"])
                chi = hi * car16
                lhs = jnp.concatenate([chi, lo * car16, chi, shi, slo, shi], 1)
                if last:
                    a = dot(lhs[:, : 5 * HD], rhs[e["h"], : 5 * HD, :HD], NN) + damping * p
                else:
                    both = dot(lhs, rhs[e["h"]], NN)
                    a, sa = both[:, :HD] + damping * p, both[:, HD:] + damping * sp
                alpha = e["n"] / (jnp.sum(p * a, axis=1, keepdims=True) + epsilon)
                e["x"] = alpha * p if it == 0 else e["x"] + alpha * p
                e["sx"] = alpha * sp if it == 0 else e["sx"] + alpha * sp
                if not last:
                    e["r"] = e["r"] - alpha * a
                    e["sr"] = e["sr"] - alpha * sa
                    new = jnp.sum(e["r"] * e["r"], axis=1, keepdims=True)
                    beta = new / (e["n"] + epsilon)
                    e["p"] = e["r"] + beta * p
                    e["sp"] = e["sr"] + beta * sp
                    e["n"] = new
        for e in state:
            h = e["h"]
            hi, lo = split2(e["x"])
            shi, slo = split2(e["sx"] * (mask_ref[...] * ksr[h : h + 1, :]))
            chi = hi * car16
            xl[h] = jnp.concatenate([chi, lo * car16, chi, shi, slo], 1)

    def finish(g):
        st = PAIRS + g
        for d in (1, 2, 3):
            ecopy(st, d).wait_recv()
        for i in range(2):
            h = 2 * g + i
            v = v_ref[:, head_cols(h)]
            cross = jnp.concatenate([ebuf[st, 2 * i], ebuf[st, 2 * i + 1]], 0)
            xhi, xlo = split2(cross)
            mixed = dot(xl[h], jnp.concatenate([xhi, xhi, xlo, v, v], 0), NN)
            inv = lax.rsqrt(jnp.sum(mixed * mixed, axis=1, keepdims=True) / HD + epsilon)
            nbuf[:, head_cols(h)] = (mixed * inv * gain_ref[...]).astype(BF16)

    half = HEADS * HD
    width = half // NB

    def columns(b):
        side = 1 - c if b < NB else c
        return pl.ds(pl.multiple_of(side * half + (b % NB) * width, width), width)

    def project(g, b):
        mine = slice(2 * HD * g, 2 * HD * (g + 1))
        return dot(nbuf[:, mine], w_ref[mine, columns(b)], NN)

    def project_pair(g):
        for b in range(2 * NB):
            acc[b] = project(g, b) if g == 0 else acc[b] + project(g, b)

    KEY.wait()
    gram_stage(0)
    pl.semaphore_wait(barrier, 7 + jnp.minimum(z, 1))

    @pl.when(z > 0)
    def _():
        pl.semaphore_signal(ready, inc=1, device_id=(s - 16, c), device_id_type=MESH)

    send_tail(0)
    for g in range(1, PAIRS):
        gram_stage(g)
        send_tail(g)
    VAL.wait()
    for g in range(PAIRS):
        cross_stage(g)
        send_tail(PAIRS + g)
    row_sum(0)
    row_sum(1)
    QUERY.wait()
    prepare(0)
    row_sum(2)
    row_sum(3)
    plane_sum(0)
    prepare(1)
    plane_sum(1)
    row_sum(4)
    plane_sum(2)
    give_back(0)
    plane_sum(3)
    row_sum(5)
    give_back(1)
    prepare(2)
    row_sum(6)
    give_back(2)
    plane_sum(4)
    give_back(3)
    prepare(3)
    row_sum(7)
    plane_sum(5)
    give_back(4)
    solve(0)
    plane_sum(6)
    give_back(5)
    plane_sum(7)
    solve(1)
    give_back(6)
    give_back(7)
    solve(2)
    solve(3)
    GAIN.wait()
    WEIGHT.wait()
    for g in range(PAIRS - 1):
        finish(g)
        project_pair(g)
    finish(PAIRS - 1)

    def pcopy(b):
        return pltpu.make_async_remote_copy(
            acc.at[b], other.at[b], ps.at[b], pr.at[b],
            device_id=(s, 1 - c), device_id_type=MESH,
        )

    for b in range(NB):
        acc[b] = acc[b] + project(PAIRS - 1, b)
        pcopy(b).start()
    for b in range(NB):
        mine = acc[NB + b] + project(PAIRS - 1, NB + b)
        pcopy(b).wait_recv()
        out_ref[:, b * width : (b + 1) * width] = (mine + other[b]).astype(BF16)

    for st in range(2 * PAIRS):
        for d in (1, 2, 3):
            ycopy(st, d).wait_send()
            xcopy(st, d).wait_send()
            ecopy(st, d).wait_send()

    @pl.when(z < LAST)
    def _():
        for st in range(2 * PAIRS):
            zcopy(st).wait_send()

    for b in range(NB):
        pcopy(b).wait_send()


def on_device(query_rows, key_rows, value_rows, doc_lengths, norm_gain, out_weight):
    half = HEADS * HD
    st = 2 * PAIRS
    dma = pltpu.SemaphoreType.DMA
    vm = pl.BlockSpec(memory_space=pltpu.VMEM)
    anywhere = pl.BlockSpec(memory_space=pl.ANY)
    return pl.pallas_call(
        kernel,
        out_shape=pltpu.VMEM((TOK, half), BF16),
        in_specs=[anywhere] * 6,
        out_specs=vm,
        scratch_shapes=[
            pltpu.VMEM((TOK, half), BF16),
            pltpu.VMEM((TOK, half), BF16),
            pltpu.VMEM((TOK, half), BF16),
            pltpu.VMEM((half, 2 * half), BF16),
            pltpu.VMEM((1, HD), jnp.int32),
            pltpu.VMEM((1, HD), F32),
            pltpu.VMEM((st, 4, CH, HD), F32),
            pltpu.VMEM((st, 4, CH, HD), F32),
            pltpu.VMEM((st, 4, CH, HD), F32),
            pltpu.VMEM((st, CH, HD), F32),
            pltpu.VMEM((st, CH, HD), F32),
            pltpu.VMEM((st, 4, CH, HD), F32),
            pltpu.VMEM((st, 4, CH, HD), F32),
            pltpu.VMEM((HEADS, TOK, HD), F32),
            pltpu.VMEM((HEADS, TOK, TOK), F32),
            pltpu.VMEM((HEADS, 6 * HD, 2 * HD), BF16),
            pltpu.VMEM((HEADS, TOK, 5 * HD), BF16),
            pltpu.VMEM((TOK, half), BF16),
            pltpu.VMEM((2 * NB, TOK, half // NB), F32),
            pltpu.VMEM((NB, TOK, half // NB), F32),
            pltpu.VMEM((TOK, TOK), F32),
            pltpu.VMEM((HEADS, HD), F32),
            pltpu.VMEM((40, HD), F32),
            pltpu.VMEM((TOK, HD), F32),
            pltpu.VMEM((TOK, HD), F32),
            dma((6,)),
            dma((st, 3)), dma((st, 3)),
            dma((st, 3)), dma((st, 3)),
            dma((st,)), dma((st,)),
            dma((st, 3)), dma((st, 3)),
            dma((NB,)), dma((NB,)),
            pltpu.SemaphoreType.REGULAR,
        ],
        compiler_params=pltpu.CompilerParams(collective_id=0, has_side_effects=True),
        name="mesa",
    )(
        query_rows, key_rows, value_rows,
        doc_lengths.reshape(1, -1), norm_gain.reshape(1, -1), out_weight,
    )


def solution(mesh):
    in_specs = (P("seq", "head"), P("seq", "head"), P("seq", "head"), P(), P(), P("head", None))
    return jax.shard_map(
        on_device, mesh=mesh, in_specs=in_specs, out_specs=P("seq", "head"), check_vma=False
    )
```

```python
import jax
import jax.numpy as jnp
from jax import lax
from jax.experimental import pallas as pl
from jax.experimental.pallas import tpu as pltpu
from jax.sharding import PartitionSpec as P

MESH = pl.DeviceIdType.MESH
F32 = jnp.float32
BF16 = jnp.bfloat16
HD = 128
TOK = 128
HEADS = 8
PAIRS = 4
ITERS = 4
CH = 64
CG = 40
CROSS = ((0, 1), (2, 3), (4, 5), (6,), (7,))
STAGES = PAIRS + len(CROSS)
LAST = 7
NB = 4
epsilon = 1e-06
damping = 1.0

WR, WZ, WC, WP, WE, WEC = 0, 4, 8, 12, 16, 32


def split2(a):
    hi = a.astype(BF16)
    return hi, (a - hi.astype(F32)).astype(BF16)


def dot(a, b, dims):
    return lax.dot_general(a, b, (dims, ((), ())), preferred_element_type=F32)


NN, NT, TN = ((1,), (0,)), ((1,), (1,)), ((0,), (0,))


def kernel(
    q_hbm, k_hbm, v_hbm, len_hbm, gain_hbm, w_hbm, out_ref,
    q_ref, k_ref, v_ref, w_ref, len_ref, gain_ref,
    tbuf, ybuf, rbuf, zs, zr, eo, ebuf, qs, scq, rhs, xl, nbuf, acc, other, obuf,
    mask_ref, ksr, wts, tail_ref, car_ref,
    lsem, ys, yr, xsd, xr, zsd, zrv, es, er, ps, pr, osem, ready,
):
    s = lax.axis_index("seq")
    c = lax.axis_index("head")
    y = lax.rem(s, 4)
    row = s - y
    x = lax.rem(s // 4, 4)
    col = s - 4 * x
    z = s // 16

    def at_y(d):
        return row + lax.rem(y + d, 4)

    def at_x(d):
        return col + 4 * lax.rem(x + d, 4)

    barrier = pltpu.get_barrier_semaphore()
    for d in (1, 2, 3):
        pl.semaphore_signal(barrier, inc=1, device_id=(at_y(d), c), device_id_type=MESH)
        pl.semaphore_signal(barrier, inc=1, device_id=(at_x(d), c), device_id_type=MESH)
    pl.semaphore_signal(barrier, inc=1, device_id=(s, 1 - c), device_id_type=MESH)

    @pl.when(z < LAST)
    def _():
        pl.semaphore_signal(barrier, inc=1, device_id=(s + 16, c), device_id_type=MESH)

    loads = [
        pltpu.make_async_copy(a, b, lsem.at[i])
        for i, (a, b) in enumerate(
            [
                (len_hbm, len_ref), (k_hbm, k_ref), (v_hbm, v_ref),
                (q_hbm, q_ref), (gain_hbm, gain_ref), (w_hbm, w_ref),
            ]
        )
    ]
    LEN, KEY, VAL, QUERY, GAIN, WEIGHT = loads
    for cp in loads:
        cp.start()

    @pl.when(z == 0)
    def _():
        zr[...] = jnp.zeros_like(zr)

    LEN.wait()
    lrow = len_ref[...].astype(F32)
    ri = lax.broadcasted_iota(jnp.int32, (TOK, TOK), 0)
    ci = lax.broadcasted_iota(jnp.int32, (TOK, TOK), 1)
    lcol = jnp.sum(jnp.where(ri == ci, lrow, 0.0), axis=1, keepdims=True)
    srow = jnp.sum(jnp.where(ri < ci, lcol, 0.0), axis=0, keepdims=True)
    scol = jnp.sum(jnp.where(ci < ri, lrow, 0.0), axis=1, keepdims=True)
    base = (s * TOK).astype(F32)
    rf, cf = ri.astype(F32), ci.astype(F32)
    doc_col = jnp.sum(jnp.where(srow <= base + rf, 1.0, 0.0), axis=1, keepdims=True)
    doc_row = jnp.sum(jnp.where(scol <= base + cf, 1.0, 0.0), axis=0, keepdims=True)
    ends = jnp.sum(jnp.where(scol <= cf * TOK + (TOK - 1.0), 1.0, 0.0), axis=0, keepdims=True)
    shard = lax.broadcasted_iota(jnp.int32, (1, TOK), 1)

    def end_of(i):
        return jnp.sum(jnp.where(shard == i, ends, 0.0), axis=1, keepdims=True)

    def put(k, flag):
        wts[k : k + 1, :] = jnp.broadcast_to(jnp.where(flag, 1.0, 0.0), (1, HD))

    here, before = end_of(s), end_of(s - 1)
    car_ref[...] = jnp.broadcast_to(jnp.where(doc_col == before, 1.0, 0.0), (TOK, HD))
    tail_ref[...] = jnp.broadcast_to(jnp.where(doc_col == here, 1.0, 0.0), (TOK, HD))
    mask_ref[...] = jnp.where((doc_col == doc_row) & (ci <= ri), 1.0, 0.0)
    dy = [end_of(row + i) for i in range(4)]
    dx = [end_of(16 * z + 4 * i + 3) for i in range(4)]
    dprev, dplane = end_of(row - 1), end_of(16 * z - 1)
    for i in range(4):
        put(WR + i, dy[i] == dy[3])
        put(WZ + i, dx[i] == dx[3])
        put(WC + i, (dx[i] == dprev) & (jnp.full((1, 1), i, jnp.int32) < x))
    put(WP, (dplane == dprev) & (dplane > 0.0))
    for t in range(1, 4):
        for i in range(t):
            put(WE + 4 * t + i, dy[i] == dy[t - 1])
        put(WEC + t, dprev == dy[t - 1])

    def wt(k):
        return wts[k : k + 1, :]

    def head_cols(h):
        return pl.ds(pl.multiple_of(h * HD, HD), HD)

    def rows(st):
        return pl.ds(0, CG if st < PAIRS else 32 * len(CROSS[st - PAIRS]))

    def kind(st):
        return 0 if st < PAIRS else 1 if len(CROSS[st - PAIRS]) == 2 else 2

    def ycopy(st, d):
        r = rows(st)
        return pltpu.make_async_remote_copy(
            tbuf.at[st, lax.rem(y + d, 4), r], ybuf.at[st, y, r], ys.at[kind(st)], yr.at[st],
            device_id=(at_y(d), c), device_id_type=MESH,
        )

    def xcopy(st, d):
        r = rows(st)
        return pltpu.make_async_remote_copy(
            rbuf.at[st, x, r], rbuf.at[st, x, r], xsd.at[kind(st)], xr.at[st],
            device_id=(at_x(d), c), device_id_type=MESH,
        )

    def zcopy(st):
        r = rows(st)
        return pltpu.make_async_remote_copy(
            zs.at[st, r], zr.at[st, r], zsd.at[kind(st)], zrv.at[st],
            device_id=(lax.rem(s + 16, 128), c), device_id_type=MESH,
        )

    def ecopy(st, d):
        r = rows(st)
        return pltpu.make_async_remote_copy(
            eo.at[st, lax.rem(y + d, 4), r], ebuf.at[st, y, r], es.at[kind(st)], er.at[st],
            device_id=(at_y(d), c), device_id_type=MESH,
        )

    def wait_bytes(ref, sem):
        pltpu.make_async_copy(ref, ref, sem).wait()

    def arrived(ref, sem, st):
        wait_bytes(ref.at[st, pl.ds(0, 3), rows(st)], sem.at[st])

    def send_tail(st):
        r = rows(st)
        for d in (1, 2, 3):
            ycopy(st, d).start()
        ybuf[st, y, r] = tbuf[st, y, r]

    lane = lax.broadcasted_iota(jnp.int32, (32, HD), 1)

    def gram_stage(g):
        grams = []
        for h in (2 * g, 2 * g + 1):
            k = k_ref[:, head_cols(h)]
            kf = k.astype(F32)
            ks = lax.rsqrt(jnp.sum(kf * kf, axis=1, keepdims=True) + epsilon)
            ksr[h : h + 1, :] = jnp.sum(jnp.where(ri == ci, ks, 0.0), axis=0, keepdims=True)
            hi, lo = split2(kf * (ks * ks) * tail_ref[...])
            grams.append(dot(jnp.concatenate([hi, lo], 0), jnp.concatenate([k, k], 0), TN))
        blocks = []
        for gram in grams:
            blocks.append(gram[:32])
            blocks.append(jnp.where(lane < 32, pltpu.roll(gram[96:], 32, 1), gram[32:64]))
        blocks.append(jnp.where(lane < 64, pltpu.roll(grams[1][64:96], 64, 1), grams[0][64:96]))
        packed = jnp.concatenate(blocks, 0)
        for o in range(4):
            tbuf[g, o, :CG] = packed[CG * o : CG * (o + 1)]

    def gram_of(g, i):
        packed = jnp.concatenate([ebuf[g, o, :CG] for o in range(4)], 0)
        first, second, third = packed[64 * i : 64 * i + 32], packed[64 * i + 32 : 64 * i + 64], packed[128:]
        if i == 1:
            third = pltpu.roll(third, 64, 1)
        upper = jnp.concatenate([first, second, third, pltpu.roll(second, 96, 1)], 0)
        return jnp.where(ci // 32 >= ri // 32, upper, upper.T)

    def cross_stage(st):
        parts = []
        for h in CROSS[st - PAIRS]:
            k = k_ref[:, head_cols(h)]
            v = v_ref[:, head_cols(h)]
            kf = k.astype(F32)
            ks = lax.rsqrt(jnp.sum(kf * kf, axis=1, keepdims=True) + epsilon)
            hi, lo = split2(kf * ks * tail_ref[...])
            parts.append(dot(jnp.concatenate([hi, lo], 0), jnp.concatenate([v, v], 0), TN))
        n = 32 * len(parts)
        stacked = jnp.concatenate(parts, 0)
        for o in range(4):
            tbuf[st, o, :n] = stacked[n * o : n * (o + 1)]

    def row_sum(st):
        r = rows(st)
        arrived(ybuf, yr, st)
        total = ybuf[st, 3, r]
        for i in range(3):
            total = total + wt(WR + i) * ybuf[st, i, r]
        rbuf[st, x, r] = total
        for d in (1, 2, 3):
            xcopy(st, d).start()

    def plane_sum(st):
        r = rows(st)
        arrived(rbuf, xr, st)
        total = rbuf[st, 3, r]
        for i in range(3):
            total = total + wt(WZ + i) * rbuf[st, i, r]
        zs[st, r] = total

        @pl.when(z < LAST)
        def _():
            if st == 0:
                pl.semaphore_wait(ready, 1)
            zcopy(st).start()

    def give_back(st):
        r = rows(st)

        @pl.when(z > 0)
        def _():
            zcopy(st).wait_recv()

        come = wt(WP) * zr[st, r]
        for i in range(3):
            come = come + wt(WC + i) * rbuf[st, i, r]
        eo[st, 0, r] = come
        parts = [ybuf[st, i, r] for i in range(3)]
        for t in range(1, 4):
            total = wt(WEC + t) * come
            for i in range(t):
                total = total + wt(WE + 4 * t + i) * parts[i]
            eo[st, t, r] = total
        for d in (1, 2, 3):
            ecopy(st, d).start()
        ebuf[st, y, r] = eo[st, y, r]

    def prepare(g):
        for h in (2 * g, 2 * g + 1):
            q = q_ref[:, head_cols(h)].astype(F32)
            qn = q * lax.rsqrt(jnp.sum(q * q, axis=1, keepdims=True) + epsilon)
            k = k_ref[:, head_cols(h)]
            hi, lo = split2(qn)
            qs[h] = qn
            scq[h] = dot(jnp.concatenate([hi, lo], 1), jnp.concatenate([k, k], 1), NT)
            khi, klo = split2(dot(k, k, NT))
            both = jnp.concatenate([k, khi], 1)
            rhs[h, 3 * HD : 4 * HD] = both
            rhs[h, 4 * HD : 5 * HD] = both
            rhs[h, 5 * HD :] = jnp.concatenate([jnp.zeros_like(klo), klo], 1)

    def solve(pairs):
        car16 = car_ref[...].astype(BF16)
        state = []
        for g, i in [(g, i) for g in pairs for i in range(2)]:
            if i == 0:
                arrived(ebuf, er, g)
            h = 2 * g + i
            k = k_ref[:, head_cols(h)]
            ghi, glo = split2(gram_of(g, i))
            shi, slo = split2(dot(jnp.concatenate([ghi, glo], 1), jnp.concatenate([k, k], 1), NT))
            both = jnp.concatenate([ghi, shi], 1)
            rhs[h, :HD] = both
            rhs[h, HD : 2 * HD] = both
            rhs[h, 2 * HD : 3 * HD] = jnp.concatenate([glo, slo], 1)
            ksrow = ksr[h : h + 1, :]
            qn, sc = qs[h], scq[h]
            state.append(
                dict(
                    h=h, m=mask_ref[...] * (ksrow * ksrow), p=qn, sp=sc, r=qn, sr=sc,
                    n=jnp.sum(qn * qn, axis=1, keepdims=True),
                )
            )
        for it in range(ITERS):
            last = it == ITERS - 1
            for e in state:
                p, sp = e["p"], e["sp"]
                hi, lo = split2(p)
                shi, slo = split2(sp * e["m"])
                chi = hi * car16
                lhs = jnp.concatenate([chi, lo * car16, chi, shi, slo, shi], 1)
                if last:
                    a = dot(lhs[:, : 5 * HD], rhs[e["h"], : 5 * HD, :HD], NN) + damping * p
                else:
                    both = dot(lhs, rhs[e["h"]], NN)
                    a, sa = both[:, :HD] + damping * p, both[:, HD:] + damping * sp
                alpha = e["n"] / (jnp.sum(p * a, axis=1, keepdims=True) + epsilon)
                e["x"] = alpha * p if it == 0 else e["x"] + alpha * p
                e["sx"] = alpha * sp if it == 0 else e["sx"] + alpha * sp
                if not last:
                    e["r"] = e["r"] - alpha * a
                    e["sr"] = e["sr"] - alpha * sa
                    new = jnp.sum(e["r"] * e["r"], axis=1, keepdims=True)
                    beta = new / (e["n"] + epsilon)
                    e["p"] = e["r"] + beta * p
                    e["sp"] = e["sr"] + beta * sp
                    e["n"] = new
            yield
        for e in state:
            h = e["h"]
            hi, lo = split2(e["x"])
            shi, slo = split2(e["sx"] * (mask_ref[...] * ksr[h : h + 1, :]))
            chi = hi * car16
            xl[h] = jnp.concatenate([chi, lo * car16, chi, shi, slo], 1)

    def finish(st):
        arrived(ebuf, er, st)
        n = 32 * len(CROSS[st - PAIRS])
        stacked = jnp.concatenate([ebuf[st, o, :n] for o in range(4)], 0)
        for i, h in enumerate(CROSS[st - PAIRS]):
            v = v_ref[:, head_cols(h)]
            xhi, xlo = split2(stacked[HD * i : HD * (i + 1)])
            mixed = dot(xl[h], jnp.concatenate([xhi, xhi, xlo, v, v], 0), NN)
            inv = lax.rsqrt(jnp.sum(mixed * mixed, axis=1, keepdims=True) / HD + epsilon)
            nbuf[:, head_cols(h)] = (mixed * inv * gain_ref[...]).astype(BF16)

    half = HEADS * HD
    width = half // NB

    def columns(b):
        side = 1 - c if b < NB else c
        return pl.ds(pl.multiple_of(side * half + (b % NB) * width, width), width)

    def project(g, b):
        mine = slice(2 * HD * g, 2 * HD * (g + 1))
        return dot(nbuf[:, mine], w_ref[mine, columns(b)], NN)

    def project_pair(g):
        for b in range(2 * NB):
            acc[b] = project(g, b) if g == 0 else acc[b] + project(g, b)

    KEY.wait()
    gram_stage(0)
    pl.semaphore_wait(barrier, 7 + jnp.minimum(z, 1))

    @pl.when(z > 0)
    def _():
        pl.semaphore_signal(ready, inc=1, device_id=(s - 16, c), device_id_type=MESH)

    send_tail(0)
    for g in range(1, PAIRS):
        gram_stage(g)
        send_tail(g)
    VAL.wait()
    for st in range(PAIRS, STAGES):
        cross_stage(st)
        send_tail(st)
    row_sum(0)
    row_sum(1)
    QUERY.wait()
    prepare(0)
    row_sum(2)
    row_sum(3)
    prepare(1)
    row_sum(4)
    plane_sum(0)
    plane_sum(1)
    row_sum(5)
    plane_sum(2)
    give_back(0)
    plane_sum(3)
    row_sum(6)
    give_back(1)
    prepare(2)
    row_sum(7)
    give_back(2)
    row_sum(8)
    plane_sum(4)
    prepare(3)
    give_back(3)
    plane_sum(5)
    give_back(4)
    first = solve((0, 1))
    next(first)
    plane_sum(6)
    give_back(5)
    next(first)
    plane_sum(7)
    plane_sum(8)
    next(first)
    give_back(6)
    next(first)
    give_back(7)
    give_back(8)
    for _ in first:
        pass
    for _ in solve((2, 3)):
        pass
    GAIN.wait()
    WEIGHT.wait()
    for g in range(PAIRS - 1):
        finish(PAIRS + g)
        project_pair(g)
    finish(7)
    finish(8)

    def pcopy(b):
        return pltpu.make_async_remote_copy(
            acc.at[b], other.at[b], ps.at[0], pr.at[b],
            device_id=(s, 1 - c), device_id_type=MESH,
        )

    def ocopy(b):
        part = (slice(None), pl.ds(b * width, width))
        return pltpu.make_async_copy(obuf.at[part], out_ref.at[part], osem.at[0])

    for b in range(NB):
        acc[b] = acc[b] + project(PAIRS - 1, b)
        pcopy(b).start()
    for b in range(NB):
        mine = acc[NB + b] + project(PAIRS - 1, NB + b)
        pcopy(b).wait_recv()
        obuf[:, b * width : (b + 1) * width] = (mine + other[b]).astype(BF16)
        ocopy(b).start()

    for i in range(3):
        group = [st for st in range(STAGES) if kind(st) == i]
        several = pl.ds(group[0], len(group))
        for ref, sem in ((ybuf, ys), (rbuf, xsd), (ebuf, es)):
            wait_bytes(ref.at[several, pl.ds(0, 3), rows(group[0])], sem.at[i])

        @pl.when(z < LAST)
        def _():
            wait_bytes(zs.at[several, rows(group[0])], zsd.at[i])

    wait_bytes(other, ps.at[0])
    wait_bytes(obuf, osem.at[0])


def on_device(query_rows, key_rows, value_rows, doc_lengths, norm_gain, out_weight):
    half = HEADS * HD
    st = STAGES
    dma = pltpu.SemaphoreType.DMA
    anywhere = pl.BlockSpec(memory_space=pl.ANY)
    return pl.pallas_call(
        kernel,
        out_shape=pltpu.VMEM((TOK, half), BF16),
        in_specs=[anywhere] * 6,
        out_specs=anywhere,
        scratch_shapes=[
            pltpu.VMEM((TOK, half), BF16),
            pltpu.VMEM((TOK, half), BF16),
            pltpu.VMEM((TOK, half), BF16),
            pltpu.VMEM((half, 2 * half), BF16),
            pltpu.VMEM((1, HD), jnp.int32),
            pltpu.VMEM((1, HD), F32),
            pltpu.VMEM((st, 4, CH, HD), F32),
            pltpu.VMEM((st, 4, CH, HD), F32),
            pltpu.VMEM((st, 4, CH, HD), F32),
            pltpu.VMEM((st, CH, HD), F32),
            pltpu.VMEM((st, CH, HD), F32),
            pltpu.VMEM((st, 4, CH, HD), F32),
            pltpu.VMEM((st, 4, CH, HD), F32),
            pltpu.VMEM((HEADS, TOK, HD), F32),
            pltpu.VMEM((HEADS, TOK, TOK), F32),
            pltpu.VMEM((HEADS, 6 * HD, 2 * HD), BF16),
            pltpu.VMEM((HEADS, TOK, 5 * HD), BF16),
            pltpu.VMEM((TOK, half), BF16),
            pltpu.VMEM((2 * NB, TOK, half // NB), F32),
            pltpu.VMEM((NB, TOK, half // NB), F32),
            pltpu.VMEM((TOK, half), BF16),
            pltpu.VMEM((TOK, TOK), F32),
            pltpu.VMEM((HEADS, HD), F32),
            pltpu.VMEM((40, HD), F32),
            pltpu.VMEM((TOK, HD), F32),
            pltpu.VMEM((TOK, HD), F32),
            dma((6,)),
            dma((3,)), dma((st,)),
            dma((3,)), dma((st,)),
            dma((3,)), dma((st,)),
            dma((3,)), dma((st,)),
            dma((1,)), dma((NB,)), dma((1,)),
            pltpu.SemaphoreType.REGULAR,
        ],
        compiler_params=pltpu.CompilerParams(collective_id=0, has_side_effects=True),
        name="mesa",
    )(
        query_rows, key_rows, value_rows,
        doc_lengths.reshape(1, -1), norm_gain.reshape(1, -1), out_weight,
    )


def solution(mesh):
    in_specs = (P("seq", "head"), P("seq", "head"), P("seq", "head"), P(), P(), P("head", None))
    return jax.shard_map(
        on_device, mesh=mesh, in_specs=in_specs, out_specs=P("seq", "head"), check_vma=False
    )
```

```python
import jax
import jax.numpy as jnp
from jax import lax
from jax.experimental import pallas as pl
from jax.experimental.pallas import tpu as pltpu
from jax.sharding import PartitionSpec as P

MESH = pl.DeviceIdType.MESH
F32 = jnp.float32
BF16 = jnp.bfloat16
HD = 128
TOK = 128
HEADS = 8
PAIRS = 4
ITERS = 4
CH = 64
CG = 40
CROSS = ((0, 1), (2, 3), (4, 5), (6,), (7,))
STAGES = PAIRS + len(CROSS)
LAST = 7
NB = 4
epsilon = 1e-06
damping = 1.0

WR, WZ, WC, WP, WE, WEC = 0, 4, 8, 12, 16, 32


def split2(a):
    hi = a.astype(BF16)
    return hi, (a - hi.astype(F32)).astype(BF16)


def dot(a, b, dims):
    return lax.dot_general(a, b, (dims, ((), ())), preferred_element_type=F32)


NN, NT, TN = ((1,), (0,)), ((1,), (1,)), ((0,), (0,))


def kernel(
    q_hbm, k_hbm, v_hbm, len_hbm, gain_hbm, w_hbm, out_ref,
    q_ref, k_ref, v_ref, w_ref, len_ref, gain_ref,
    tbuf, ybuf, rbuf, zs, zr, eo, ebuf, qs, scq, lhs, xl, vt, mf, mg, nbuf, acc, other, obuf,
    mask_ref, wts, tail_ref, car_ref,
    lsem, sent, yr, xr, zsd, zrv, er, ps, pr, osem, ready,
):
    s = lax.axis_index("seq")
    c = lax.axis_index("head")
    y = lax.rem(s, 4)
    row = s - y
    x = lax.rem(s // 4, 4)
    col = s - 4 * x
    z = s // 16

    def at_y(d):
        return row + lax.rem(y + d, 4)

    def at_x(d):
        return col + 4 * lax.rem(x + d, 4)

    barrier = pltpu.get_barrier_semaphore()
    for d in (1, 2, 3):
        pl.semaphore_signal(barrier, inc=1, device_id=(at_y(d), c), device_id_type=MESH)
        pl.semaphore_signal(barrier, inc=1, device_id=(at_x(d), c), device_id_type=MESH)
    pl.semaphore_signal(barrier, inc=1, device_id=(s, 1 - c), device_id_type=MESH)

    @pl.when(z < LAST)
    def _():
        pl.semaphore_signal(barrier, inc=1, device_id=(s + 16, c), device_id_type=MESH)

    loads = [
        pltpu.make_async_copy(a, b, lsem.at[i])
        for i, (a, b) in enumerate(
            [
                (len_hbm, len_ref), (k_hbm, k_ref), (v_hbm, v_ref),
                (q_hbm, q_ref), (gain_hbm, gain_ref), (w_hbm, w_ref),
            ]
        )
    ]
    LEN, KEY, VAL, QUERY, GAIN, WEIGHT = loads
    for cp in loads:
        cp.start()

    @pl.when(z == 0)
    def _():
        zr[...] = jnp.zeros_like(zr)

    LEN.wait()
    lrow = len_ref[...].astype(F32)
    ri = lax.broadcasted_iota(jnp.int32, (TOK, TOK), 0)
    ci = lax.broadcasted_iota(jnp.int32, (TOK, TOK), 1)
    lcol = jnp.sum(jnp.where(ri == ci, lrow, 0.0), axis=1, keepdims=True)
    srow = jnp.sum(jnp.where(ri < ci, lcol, 0.0), axis=0, keepdims=True)
    scol = jnp.sum(jnp.where(ci < ri, lrow, 0.0), axis=1, keepdims=True)
    base = (s * TOK).astype(F32)
    rf, cf = ri.astype(F32), ci.astype(F32)
    doc_col = jnp.sum(jnp.where(srow <= base + rf, 1.0, 0.0), axis=1, keepdims=True)
    doc_row = jnp.sum(jnp.where(scol <= base + cf, 1.0, 0.0), axis=0, keepdims=True)
    ends = jnp.sum(jnp.where(scol <= cf * TOK + (TOK - 1.0), 1.0, 0.0), axis=0, keepdims=True)
    shard = lax.broadcasted_iota(jnp.int32, (1, TOK), 1)

    def end_of(i):
        return jnp.sum(jnp.where(shard == i, ends, 0.0), axis=1, keepdims=True)

    def put(k, flag):
        wts[k : k + 1, :] = jnp.broadcast_to(jnp.where(flag, 1.0, 0.0), (1, HD))

    here, before = end_of(s), end_of(s - 1)
    car_ref[...] = jnp.where(doc_row == before, 1.0, 0.0)
    tail_ref[...] = jnp.broadcast_to(jnp.where(doc_col == here, 1.0, 0.0), (TOK, HD))
    mask_ref[...] = jnp.where((doc_col == doc_row) & (ri <= ci), 1.0, 0.0)
    dy = [end_of(row + i) for i in range(4)]
    dx = [end_of(16 * z + 4 * i + 3) for i in range(4)]
    dprev, dplane = end_of(row - 1), end_of(16 * z - 1)
    for i in range(4):
        put(WR + i, dy[i] == dy[3])
        put(WZ + i, dx[i] == dx[3])
        put(WC + i, (dx[i] == dprev) & (jnp.full((1, 1), i, jnp.int32) < x))
    put(WP, (dplane == dprev) & (dplane > 0.0))
    for t in range(1, 4):
        for i in range(t):
            put(WE + 4 * t + i, dy[i] == dy[t - 1])
        put(WEC + t, dprev == dy[t - 1])

    def wt(k):
        return wts[k : k + 1, :]

    def head_cols(h):
        return pl.ds(pl.multiple_of(h * HD, HD), HD)

    def rows(st):
        return pl.ds(0, CG if st < PAIRS else 32 * len(CROSS[st - PAIRS]))

    def kind(st):
        return 0 if st < PAIRS else 1 if len(CROSS[st - PAIRS]) == 2 else 2

    def ycopy(st, d):
        r = rows(st)
        return pltpu.make_async_remote_copy(
            tbuf.at[st, lax.rem(y + d, 4), r], ybuf.at[st, y, r], sent.at[kind(st)], yr.at[st],
            device_id=(at_y(d), c), device_id_type=MESH,
        )

    def xcopy(st, d):
        r = rows(st)
        return pltpu.make_async_remote_copy(
            rbuf.at[st, x, r], rbuf.at[st, x, r], sent.at[kind(st)], xr.at[st],
            device_id=(at_x(d), c), device_id_type=MESH,
        )

    def zcopy(st):
        r = rows(st)
        return pltpu.make_async_remote_copy(
            zs.at[st, r], zr.at[st, r], zsd.at[kind(st)], zrv.at[st],
            device_id=(lax.rem(s + 16, 128), c), device_id_type=MESH,
        )

    def ecopy(st, d):
        r = rows(st)
        return pltpu.make_async_remote_copy(
            eo.at[st, lax.rem(y + d, 4), r], ebuf.at[st, y, r], sent.at[kind(st)], er.at[st],
            device_id=(at_y(d), c), device_id_type=MESH,
        )

    def wait_bytes(ref, sem):
        pltpu.make_async_copy(ref, ref, sem).wait()

    def arrived(ref, sem, st):
        wait_bytes(ref.at[st, pl.ds(0, 3), rows(st)], sem.at[st])

    def send_tail(st):
        r = rows(st)
        for d in (1, 2, 3):
            ycopy(st, d).start()
        ybuf[st, y, r] = tbuf[st, y, r]

    lane = lax.broadcasted_iota(jnp.int32, (32, HD), 1)

    def gram_stage(g):
        grams = []
        for h in (2 * g, 2 * g + 1):
            k = k_ref[:, head_cols(h)]
            kf = k.astype(F32)
            ks = lax.rsqrt(jnp.sum(kf * kf, axis=1, keepdims=True) + epsilon)
            hi, lo = split2(kf * (ks * ks) * tail_ref[...])
            grams.append(dot(jnp.concatenate([hi, lo], 0), jnp.concatenate([k, k], 0), TN))
        blocks = []
        for gram in grams:
            blocks.append(gram[:32])
            blocks.append(jnp.where(lane < 32, pltpu.roll(gram[96:], 32, 1), gram[32:64]))
        blocks.append(jnp.where(lane < 64, pltpu.roll(grams[1][64:96], 64, 1), grams[0][64:96]))
        packed = jnp.concatenate(blocks, 0)
        for o in range(4):
            tbuf[g, o, :CG] = packed[CG * o : CG * (o + 1)]

    def gram_of(g, i):
        packed = jnp.concatenate([ebuf[g, o, :CG] for o in range(4)], 0)
        first, second, third = packed[64 * i : 64 * i + 32], packed[64 * i + 32 : 64 * i + 64], packed[128:]
        if i == 1:
            third = pltpu.roll(third, 64, 1)
        upper = jnp.concatenate([first, second, third, pltpu.roll(second, 96, 1)], 0)
        return jnp.where(ci // 32 >= ri // 32, upper, upper.T)

    def cross_stage(st):
        parts = []
        for h in CROSS[st - PAIRS]:
            k = k_ref[:, head_cols(h)]
            v = v_ref[:, head_cols(h)]
            kf = k.astype(F32)
            ks = lax.rsqrt(jnp.sum(kf * kf, axis=1, keepdims=True) + epsilon)
            hi, lo = split2(kf * ks * tail_ref[...])
            parts.append(dot(jnp.concatenate([v, v], 0), jnp.concatenate([hi, lo], 0), TN))
        n = 32 * len(parts)
        stacked = jnp.concatenate(parts, 0)
        for o in range(4):
            tbuf[st, o, :n] = stacked[n * o : n * (o + 1)]

    def row_sum(st):
        r = rows(st)
        arrived(ybuf, yr, st)
        total = ybuf[st, 3, r]
        for i in range(3):
            total = total + wt(WR + i) * ybuf[st, i, r]
        rbuf[st, x, r] = total
        for d in (1, 2, 3):
            xcopy(st, d).start()

    def plane_sum(st):
        r = rows(st)
        arrived(rbuf, xr, st)
        total = rbuf[st, 3, r]
        for i in range(3):
            total = total + wt(WZ + i) * rbuf[st, i, r]
        zs[st, r] = total

        @pl.when(z < LAST)
        def _():
            if st == 0:
                pl.semaphore_wait(ready, 1)
            zcopy(st).start()

    def give_back(st):
        r = rows(st)

        @pl.when(z > 0)
        def _():
            zcopy(st).wait_recv()

        come = wt(WP) * zr[st, r]
        for i in range(3):
            come = come + wt(WC + i) * rbuf[st, i, r]
        eo[st, 0, r] = come
        parts = [ybuf[st, i, r] for i in range(3)]
        for t in range(1, 4):
            total = wt(WEC + t) * come
            for i in range(t):
                total = total + wt(WE + 4 * t + i) * parts[i]
            eo[st, t, r] = total
        for d in (1, 2, 3):
            ecopy(st, d).start()
        ebuf[st, y, r] = eo[st, y, r]

    def prepare(g):
        for h in (2 * g, 2 * g + 1):
            q = q_ref[:, head_cols(h)].astype(F32).T
            q = q * lax.rsqrt(jnp.sum(q * q, axis=0, keepdims=True) + epsilon)
            k = k_ref[:, head_cols(h)]
            kf = k.astype(F32)
            ks = lax.rsqrt(jnp.sum(kf * kf, axis=1, keepdims=True) + epsilon)
            m = mask_ref[...] * ks
            mf[h] = m
            mg[h] = m * ks
            hi, lo = split2(q)
            qs[h] = q
            scq[h] = dot(jnp.concatenate([k, k], 1), jnp.concatenate([hi, lo], 0), NN)
            khi, klo = split2(dot(k, k, NT))
            lhs[h, :HD, HD : 2 * HD] = kf.T.astype(BF16)
            lhs[h, HD:, HD : 2 * HD] = khi
            lhs[h, :HD, 3 * HD :] = jnp.zeros_like(klo)
            lhs[h, HD:, 3 * HD :] = klo
            vt[h] = v_ref[:, head_cols(h)].astype(F32).T.astype(BF16)

    def columns_of(vector, scores):
        hi, lo = split2(vector)
        shi, slo = split2(scores)
        car16 = car_ref[...].astype(BF16)
        return jnp.concatenate([hi * car16, shi], 0), jnp.concatenate([lo * car16, slo], 0)

    def solve(pairs):
        state = []
        for g, i in [(g, i) for g in pairs for i in range(2)]:
            if i == 0:
                arrived(ebuf, er, g)
            h = 2 * g + i
            k = k_ref[:, head_cols(h)]
            ghi, glo = split2(gram_of(g, i))
            shi, slo = split2(dot(jnp.concatenate([k, k], 1), jnp.concatenate([ghi, glo], 0), NN))
            lhs[h, :HD, :HD] = ghi
            lhs[h, HD:, :HD] = shi
            lhs[h, :HD, 2 * HD : 3 * HD] = glo
            lhs[h, HD:, 2 * HD : 3 * HD] = slo
            q, sc = qs[h], scq[h]
            n = jnp.sum(q * q, axis=0, keepdims=True)
            state.append(dict(h=h, p=q, sp=sc, r=q, sr=sc, n=n))
        yield
        for it in range(ITERS):
            last = it == ITERS - 1
            rows_here = HD if last else 2 * HD
            for e in state:
                p, sp, h = e["p"], e["sp"], e["h"]
                hi, lo = columns_of(p, sp * mg[h])
                both = dot(lhs[h, :rows_here, : 2 * HD], jnp.concatenate([hi, lo], 1), NN)
                both = both[:, :TOK] + both[:, TOK:] + dot(lhs[h, :rows_here, 2 * HD :], hi, NN)
                a = both[:HD] + damping * p
                alpha = e["n"] / (jnp.sum(p * a, axis=0, keepdims=True) + epsilon)
                e["x"] = alpha * p if it == 0 else e["x"] + alpha * p
                e["sx"] = alpha * sp if it == 0 else e["sx"] + alpha * sp
                if not last:
                    sa = both[HD:] + damping * sp
                    e["r"] = e["r"] - alpha * a
                    e["sr"] = e["sr"] - alpha * sa
                    new = jnp.sum(e["r"] * e["r"], axis=0, keepdims=True)
                    beta = new / (e["n"] + epsilon)
                    e["p"] = e["r"] + beta * p
                    e["sp"] = e["sr"] + beta * sp
                    e["n"] = new
            yield
        for e in state:
            h = e["h"]
            hi, lo = columns_of(e["x"], e["sx"] * mf[h])
            xl[h] = jnp.concatenate([hi, lo], 1)

    def finish(*stages):
        for st in stages:
            arrived(ebuf, er, st)
        states = []
        for st in stages:
            n = 32 * len(CROSS[st - PAIRS])
            stacked = jnp.concatenate([ebuf[st, o, :n] for o in range(4)], 0)
            for i, h in enumerate(CROSS[st - PAIRS]):
                states.append((h, stacked[HD * i : HD * (i + 1)]))
        for h, cross in states:
            xhi, xlo = split2(cross)
            mixed = dot(jnp.concatenate([xhi, vt[h]], 1), xl[h], NN)
            mixed = mixed[:, :TOK] + mixed[:, TOK:] + dot(xlo, xl[h, :HD, :TOK], NN)
            inv = lax.rsqrt(jnp.sum(mixed * mixed, axis=0, keepdims=True) / HD + epsilon)
            nbuf[:, head_cols(h)] = (mixed * inv * gain_col()).T.astype(BF16)

    def gain_col():
        return jnp.sum(jnp.where(ri == ci, gain_ref[...], 0.0), axis=1, keepdims=True)

    half = HEADS * HD
    width = half // NB

    def columns(b):
        side = 1 - c if b < NB else c
        return pl.ds(pl.multiple_of(side * half + (b % NB) * width, width), width)

    def project(g, b):
        mine = slice(2 * HD * g, 2 * HD * (g + 1))
        return dot(nbuf[:, mine], w_ref[mine, columns(b)], NN)

    def project_pair(g):
        for b in range(2 * NB):
            acc[b] = project(g, b) if g == 0 else acc[b] + project(g, b)

    KEY.wait()
    gram_stage(0)
    pl.semaphore_wait(barrier, 7 + jnp.minimum(z, 1))

    @pl.when(z > 0)
    def _():
        pl.semaphore_signal(ready, inc=1, device_id=(s - 16, c), device_id_type=MESH)

    send_tail(0)
    for g in range(1, PAIRS):
        gram_stage(g)
        send_tail(g)
    VAL.wait()
    for st in range(PAIRS, STAGES):
        cross_stage(st)
        send_tail(st)
    row_sum(0)
    row_sum(1)
    QUERY.wait()
    prepare(0)
    row_sum(2)
    row_sum(3)
    prepare(1)
    row_sum(4)
    plane_sum(0)
    plane_sum(1)
    row_sum(5)
    plane_sum(2)
    give_back(0)
    plane_sum(3)
    row_sum(6)
    give_back(1)
    prepare(2)
    row_sum(7)
    give_back(2)
    row_sum(8)
    plane_sum(4)
    prepare(3)
    give_back(3)
    plane_sum(5)
    give_back(4)
    plane_sum(6)
    first = solve((0, 1))
    next(first)
    next(first)
    give_back(5)
    plane_sum(7)
    plane_sum(8)
    next(first)
    next(first)
    give_back(6)
    for _ in first:
        pass
    second = solve((2, 3))
    next(second)
    give_back(7)
    give_back(8)
    for _ in second:
        pass
    GAIN.wait()
    WEIGHT.wait()
    for g in range(PAIRS - 1):
        finish(PAIRS + g)
        project_pair(g)
    finish(7, 8)

    def pcopy(b):
        return pltpu.make_async_remote_copy(
            acc.at[b], other.at[b], ps.at[0], pr.at[b],
            device_id=(s, 1 - c), device_id_type=MESH,
        )

    def ocopy(b):
        part = (slice(None), pl.ds(b * width, width))
        return pltpu.make_async_copy(obuf.at[part], out_ref.at[part], osem.at[0])

    for b in range(0, NB, 2):
        for e in (b, b + 1):
            acc[e] = acc[e] + project(PAIRS - 1, e)
        for e in (b, b + 1):
            pcopy(e).start()
    for b in range(NB, 2 * NB):
        acc[b] = acc[b] + project(PAIRS - 1, b)
    for b in range(NB):
        pcopy(b).wait_recv()
        obuf[:, b * width : (b + 1) * width] = (acc[NB + b] + other[b]).astype(BF16)
        ocopy(b).start()

    for i, (stages, slots) in enumerate(((9, 4), (9, 3), (6, 3))):
        group = [st for st in range(STAGES) if kind(st) == i]
        wait_bytes(ybuf.at[pl.ds(0, stages), pl.ds(0, slots), rows(group[0])], sent.at[i])

        @pl.when(z < LAST)
        def _():
            wait_bytes(zs.at[pl.ds(group[0], len(group)), rows(group[0])], zsd.at[i])

    wait_bytes(other, ps.at[0])
    wait_bytes(obuf, osem.at[0])


def on_device(query_rows, key_rows, value_rows, doc_lengths, norm_gain, out_weight):
    half = HEADS * HD
    st = STAGES
    dma = pltpu.SemaphoreType.DMA
    anywhere = pl.BlockSpec(memory_space=pl.ANY)
    return pl.pallas_call(
        kernel,
        out_shape=pltpu.VMEM((TOK, half), BF16),
        in_specs=[anywhere] * 6,
        out_specs=anywhere,
        scratch_shapes=[
            pltpu.VMEM((TOK, half), BF16),
            pltpu.VMEM((TOK, half), BF16),
            pltpu.VMEM((TOK, half), BF16),
            pltpu.VMEM((half, 2 * half), BF16),
            pltpu.VMEM((1, HD), jnp.int32),
            pltpu.VMEM((1, HD), F32),
            pltpu.VMEM((st, 4, CH, HD), F32),
            pltpu.VMEM((st, 4, CH, HD), F32),
            pltpu.VMEM((st, 4, CH, HD), F32),
            pltpu.VMEM((st, CH, HD), F32),
            pltpu.VMEM((st, CH, HD), F32),
            pltpu.VMEM((st, 4, CH, HD), F32),
            pltpu.VMEM((st, 4, CH, HD), F32),
            pltpu.VMEM((HEADS, TOK, HD), F32),
            pltpu.VMEM((HEADS, TOK, TOK), F32),
            pltpu.VMEM((HEADS, 2 * HD, 4 * HD), BF16),
            pltpu.VMEM((HEADS, 2 * HD, 2 * TOK), BF16),
            pltpu.VMEM((HEADS, HD, TOK), BF16),
            pltpu.VMEM((HEADS, TOK, TOK), F32),
            pltpu.VMEM((HEADS, TOK, TOK), F32),
            pltpu.VMEM((TOK, half), BF16),
            pltpu.VMEM((2 * NB, TOK, half // NB), F32),
            pltpu.VMEM((NB, TOK, half // NB), F32),
            pltpu.VMEM((TOK, half), BF16),
            pltpu.VMEM((TOK, TOK), F32),
            pltpu.VMEM((40, HD), F32),
            pltpu.VMEM((TOK, HD), F32),
            pltpu.VMEM((1, TOK), F32),
            dma((6,)),
            dma((3,)), dma((st,)), dma((st,)),
            dma((3,)), dma((st,)), dma((st,)),
            dma((1,)), dma((NB,)), dma((1,)),
            pltpu.SemaphoreType.REGULAR,
        ],
        compiler_params=pltpu.CompilerParams(collective_id=0, has_side_effects=True),
        name="mesa",
    )(
        query_rows, key_rows, value_rows,
        doc_lengths.reshape(1, -1), norm_gain.reshape(1, -1), out_weight,
    )


def solution(mesh):
    in_specs = (P("seq", "head"), P("seq", "head"), P("seq", "head"), P(), P(), P("head", None))
    return jax.shard_map(
        on_device, mesh=mesh, in_specs=in_specs, out_specs=P("seq", "head"), check_vma=False
    )
```

```python
import jax
import jax.numpy as jnp
from jax import lax
from jax.experimental import pallas as pl
from jax.experimental.pallas import tpu as pltpu
from jax.sharding import PartitionSpec as P

MESH = pl.DeviceIdType.MESH
F32 = jnp.float32
BF16 = jnp.bfloat16
HD = 128
TOK = 128
HEADS = 8
PAIRS = 4
ITERS = 4
CH = 64
CG = 40
CROSS = ((0, 1), (2, 3), (4, 5), (6,), (7,))
STAGES = PAIRS + len(CROSS)
LAST = 7
NB = 4
epsilon = 1e-06
damping = 1.0

WR, WZ, WC, WP, WE, WEC = 0, 4, 8, 12, 16, 32


def split2(a):
    hi = a.astype(BF16)
    return hi, (a - hi.astype(F32)).astype(BF16)


def dot(a, b, dims):
    return lax.dot_general(a, b, (dims, ((), ())), preferred_element_type=F32)


NN, NT, TN = ((1,), (0,)), ((1,), (1,)), ((0,), (0,))


def kernel(
    q_hbm, k_hbm, v_hbm, len_hbm, gain_hbm, w_hbm, out_ref,
    q_ref, k_ref, v_ref, w_ref, len_ref, gain_ref,
    tbuf, ybuf, rbuf, zs, zr, eo, ebuf, qs, scq, lhs, xl, vt, mf, mg, nbuf, acc, other,
    mask_ref, wts, tail_ref, car_ref,
    lsem, sent, yr, xr, zsd, zrv, er, ps, pr, ready,
):
    s = lax.axis_index("seq")
    c = lax.axis_index("head")
    y = lax.rem(s, 4)
    row = s - y
    x = lax.rem(s // 4, 4)
    col = s - 4 * x
    z = s // 16

    def at_y(d):
        return row + lax.rem(y + d, 4)

    def at_x(d):
        return col + 4 * lax.rem(x + d, 4)

    barrier = pltpu.get_barrier_semaphore()
    for d in (1, 2, 3):
        pl.semaphore_signal(barrier, inc=1, device_id=(at_y(d), c), device_id_type=MESH)
        pl.semaphore_signal(barrier, inc=1, device_id=(at_x(d), c), device_id_type=MESH)
    pl.semaphore_signal(barrier, inc=1, device_id=(s, 1 - c), device_id_type=MESH)

    @pl.when(z < LAST)
    def _():
        pl.semaphore_signal(barrier, inc=1, device_id=(s + 16, c), device_id_type=MESH)

    loads = [
        pltpu.make_async_copy(a, b, lsem.at[i])
        for i, (a, b) in enumerate(
            [
                (len_hbm, len_ref), (k_hbm, k_ref), (v_hbm, v_ref),
                (q_hbm, q_ref), (gain_hbm, gain_ref), (w_hbm, w_ref),
            ]
        )
    ]
    LEN, KEY, VAL, QUERY, GAIN, WEIGHT = loads
    for cp in loads:
        cp.start()

    @pl.when(z == 0)
    def _():
        zr[...] = jnp.zeros_like(zr)

    LEN.wait()
    lrow = len_ref[...].astype(F32)
    ri = lax.broadcasted_iota(jnp.int32, (TOK, TOK), 0)
    ci = lax.broadcasted_iota(jnp.int32, (TOK, TOK), 1)
    lcol = jnp.sum(jnp.where(ri == ci, lrow, 0.0), axis=1, keepdims=True)
    srow = jnp.sum(jnp.where(ri < ci, lcol, 0.0), axis=0, keepdims=True)
    scol = jnp.sum(jnp.where(ci < ri, lrow, 0.0), axis=1, keepdims=True)
    base = (s * TOK).astype(F32)
    rf, cf = ri.astype(F32), ci.astype(F32)
    doc_col = jnp.sum(jnp.where(srow <= base + rf, 1.0, 0.0), axis=1, keepdims=True)
    doc_row = jnp.sum(jnp.where(scol <= base + cf, 1.0, 0.0), axis=0, keepdims=True)
    ends = jnp.sum(jnp.where(scol <= cf * TOK + (TOK - 1.0), 1.0, 0.0), axis=0, keepdims=True)
    shard = lax.broadcasted_iota(jnp.int32, (1, TOK), 1)

    def end_of(i):
        return jnp.sum(jnp.where(shard == i, ends, 0.0), axis=1, keepdims=True)

    def put(k, flag):
        wts[k : k + 1, :] = jnp.broadcast_to(jnp.where(flag, 1.0, 0.0), (1, HD))

    here, before = end_of(s), end_of(s - 1)
    car_ref[...] = jnp.where(doc_row == before, 1.0, 0.0)
    tail_ref[...] = jnp.broadcast_to(jnp.where(doc_col == here, 1.0, 0.0), (TOK, HD))
    mask_ref[...] = jnp.where((doc_col == doc_row) & (ri <= ci), 1.0, 0.0)
    dy = [end_of(row + i) for i in range(4)]
    dx = [end_of(16 * z + 4 * i + 3) for i in range(4)]
    dprev, dplane = end_of(row - 1), end_of(16 * z - 1)
    for i in range(4):
        put(WR + i, dy[i] == dy[3])
        put(WZ + i, dx[i] == dx[3])
        put(WC + i, (dx[i] == dprev) & (jnp.full((1, 1), i, jnp.int32) < x))
    put(WP, (dplane == dprev) & (dplane > 0.0))
    for t in range(1, 4):
        for i in range(t):
            put(WE + 4 * t + i, dy[i] == dy[t - 1])
        put(WEC + t, dprev == dy[t - 1])

    def wt(k):
        return wts[k : k + 1, :]

    def head_cols(h):
        return pl.ds(pl.multiple_of(h * HD, HD), HD)

    def rows(st):
        return pl.ds(0, CG if st < PAIRS else 32 * len(CROSS[st - PAIRS]))

    def kind(st):
        return 0 if st < PAIRS else 1 if len(CROSS[st - PAIRS]) == 2 else 2

    def ycopy(st, d):
        r = rows(st)
        return pltpu.make_async_remote_copy(
            tbuf.at[st, lax.rem(y + d, 4), r], ybuf.at[st, y, r], sent.at[kind(st)], yr.at[st],
            device_id=(at_y(d), c), device_id_type=MESH,
        )

    def xcopy(st, d):
        r = rows(st)
        return pltpu.make_async_remote_copy(
            rbuf.at[st, x, r], rbuf.at[st, x, r], sent.at[kind(st)], xr.at[st],
            device_id=(at_x(d), c), device_id_type=MESH,
        )

    def zcopy(st):
        r = rows(st)
        return pltpu.make_async_remote_copy(
            zs.at[st, r], zr.at[st, r], zsd.at[kind(st)], zrv.at[st],
            device_id=(lax.rem(s + 16, 128), c), device_id_type=MESH,
        )

    def ecopy(st, d):
        r = rows(st)
        return pltpu.make_async_remote_copy(
            eo.at[st, lax.rem(y + d, 4), r], ebuf.at[st, y, r], sent.at[kind(st)], er.at[st],
            device_id=(at_y(d), c), device_id_type=MESH,
        )

    def wait_bytes(ref, sem):
        pltpu.make_async_copy(ref, ref, sem).wait()

    def arrived(ref, sem, st):
        wait_bytes(ref.at[st, pl.ds(0, 3), rows(st)], sem.at[st])

    def send_tail(st):
        r = rows(st)
        for d in (2, 1, 3):
            ycopy(st, d).start()
        ybuf[st, y, r] = tbuf[st, y, r]

    lane = lax.broadcasted_iota(jnp.int32, (32, HD), 1)

    def gram_stage(g):
        grams = []
        for h in (2 * g, 2 * g + 1):
            k = k_ref[:, head_cols(h)]
            kf = k.astype(F32)
            ks = lax.rsqrt(jnp.sum(kf * kf, axis=1, keepdims=True) + epsilon)
            hi, lo = split2(kf * (ks * ks) * tail_ref[...])
            grams.append(dot(jnp.concatenate([hi, lo], 0), jnp.concatenate([k, k], 0), TN))
        blocks = []
        for gram in grams:
            blocks.append(gram[:32])
            blocks.append(jnp.where(lane < 32, pltpu.roll(gram[96:], 32, 1), gram[32:64]))
        blocks.append(jnp.where(lane < 64, pltpu.roll(grams[1][64:96], 64, 1), grams[0][64:96]))
        packed = jnp.concatenate(blocks, 0)
        for o in range(4):
            tbuf[g, o, :CG] = packed[CG * o : CG * (o + 1)]

    def gram_of(g, i):
        packed = jnp.concatenate([ebuf[g, o, :CG] for o in range(4)], 0)
        first, second, third = packed[64 * i : 64 * i + 32], packed[64 * i + 32 : 64 * i + 64], packed[128:]
        if i == 1:
            third = pltpu.roll(third, 64, 1)
        upper = jnp.concatenate([first, second, third, pltpu.roll(second, 96, 1)], 0)
        return jnp.where(ci // 32 >= ri // 32, upper, upper.T)

    def cross_stage(st):
        parts = []
        for h in CROSS[st - PAIRS]:
            k = k_ref[:, head_cols(h)]
            v = v_ref[:, head_cols(h)]
            kf = k.astype(F32)
            ks = lax.rsqrt(jnp.sum(kf * kf, axis=1, keepdims=True) + epsilon)
            hi, lo = split2(kf * ks * tail_ref[...])
            parts.append(dot(jnp.concatenate([v, v], 0), jnp.concatenate([hi, lo], 0), TN))
        n = 32 * len(parts)
        stacked = jnp.concatenate(parts, 0)
        for o in range(4):
            tbuf[st, o, :n] = stacked[n * o : n * (o + 1)]

    def row_sum(st):
        r = rows(st)
        arrived(ybuf, yr, st)
        total = ybuf[st, 3, r]
        for i in range(3):
            total = total + wt(WR + i) * ybuf[st, i, r]
        rbuf[st, x, r] = total
        for d in (2, 1, 3):
            xcopy(st, d).start()

    def plane_sum(st):
        r = rows(st)
        arrived(rbuf, xr, st)
        total = rbuf[st, 3, r]
        for i in range(3):
            total = total + wt(WZ + i) * rbuf[st, i, r]
        zs[st, r] = total

        @pl.when(z < LAST)
        def _():
            if st == 0:
                pl.semaphore_wait(ready, 1)
            zcopy(st).start()

    def give_back(st):
        r = rows(st)

        @pl.when(z > 0)
        def _():
            zcopy(st).wait_recv()

        come = wt(WP) * zr[st, r]
        for i in range(3):
            come = come + wt(WC + i) * rbuf[st, i, r]
        eo[st, 0, r] = come
        parts = [ybuf[st, i, r] for i in range(3)]
        for t in range(1, 4):
            total = wt(WEC + t) * come
            for i in range(t):
                total = total + wt(WE + 4 * t + i) * parts[i]
            eo[st, t, r] = total
        for d in (2, 1, 3):
            ecopy(st, d).start()
        ebuf[st, y, r] = eo[st, y, r]

    def prepare(g):
        for h in (2 * g, 2 * g + 1):
            q = q_ref[:, head_cols(h)].astype(F32).T
            q = q * lax.rsqrt(jnp.sum(q * q, axis=0, keepdims=True) + epsilon)
            k = k_ref[:, head_cols(h)]
            kf = k.astype(F32)
            ks = lax.rsqrt(jnp.sum(kf * kf, axis=1, keepdims=True) + epsilon)
            m = mask_ref[...] * ks
            mf[h] = m
            mg[h] = m * ks
            hi, lo = split2(q)
            qs[h] = q
            scq[h] = dot(jnp.concatenate([k, k], 1), jnp.concatenate([hi, lo], 0), NN)
            khi, klo = split2(dot(k, k, NT))
            lhs[h, :HD, HD : 2 * HD] = kf.T.astype(BF16)
            lhs[h, HD:, HD : 2 * HD] = khi
            lhs[h, :HD, 3 * HD :] = jnp.zeros_like(klo)
            lhs[h, HD:, 3 * HD :] = klo
            vt[h] = v_ref[:, head_cols(h)].astype(F32).T.astype(BF16)

    def columns_of(vector, scores):
        hi, lo = split2(vector)
        shi, slo = split2(scores)
        car16 = car_ref[...].astype(BF16)
        return jnp.concatenate([hi * car16, shi], 0), jnp.concatenate([lo * car16, slo], 0)

    def solve(pairs):
        state = []
        for g, i in [(g, i) for g in pairs for i in range(2)]:
            if i == 0:
                arrived(ebuf, er, g)
            h = 2 * g + i
            k = k_ref[:, head_cols(h)]
            ghi, glo = split2(gram_of(g, i))
            shi, slo = split2(dot(jnp.concatenate([k, k], 1), jnp.concatenate([ghi, glo], 0), NN))
            lhs[h, :HD, :HD] = ghi
            lhs[h, HD:, :HD] = shi
            lhs[h, :HD, 2 * HD : 3 * HD] = glo
            lhs[h, HD:, 2 * HD : 3 * HD] = slo
            q, sc = qs[h], scq[h]
            n = jnp.sum(q * q, axis=0, keepdims=True)
            state.append(dict(h=h, p=q, sp=sc, r=q, sr=sc, n=n))
        yield
        for it in range(ITERS):
            last = it == ITERS - 1
            rows_here = HD if last else 2 * HD
            for e in state:
                p, sp, h = e["p"], e["sp"], e["h"]
                hi, lo = columns_of(p, sp * mg[h])
                both = dot(lhs[h, :rows_here, : 2 * HD], jnp.concatenate([hi, lo], 1), NN)
                both = both[:, :TOK] + both[:, TOK:] + dot(lhs[h, :rows_here, 2 * HD :], hi, NN)
                a = both[:HD] + damping * p
                alpha = e["n"] / (jnp.sum(p * a, axis=0, keepdims=True) + epsilon)
                e["x"] = alpha * p if it == 0 else e["x"] + alpha * p
                e["sx"] = alpha * sp if it == 0 else e["sx"] + alpha * sp
                if not last:
                    sa = both[HD:] + damping * sp
                    e["r"] = e["r"] - alpha * a
                    e["sr"] = e["sr"] - alpha * sa
                    new = jnp.sum(e["r"] * e["r"], axis=0, keepdims=True)
                    beta = new / (e["n"] + epsilon)
                    e["p"] = e["r"] + beta * p
                    e["sp"] = e["sr"] + beta * sp
                    e["n"] = new
            yield
        for e in state:
            h = e["h"]
            hi, lo = columns_of(e["x"], e["sx"] * mf[h])
            xl[h] = jnp.concatenate([hi, lo], 1)

    def finish(*stages):
        for st in stages:
            arrived(ebuf, er, st)
        states = []
        for st in stages:
            n = 32 * len(CROSS[st - PAIRS])
            stacked = jnp.concatenate([ebuf[st, o, :n] for o in range(4)], 0)
            for i, h in enumerate(CROSS[st - PAIRS]):
                states.append((h, stacked[HD * i : HD * (i + 1)]))
        for h, cross in states:
            xhi, xlo = split2(cross)
            mixed = dot(jnp.concatenate([xhi, vt[h]], 1), xl[h], NN)
            mixed = mixed[:, :TOK] + mixed[:, TOK:] + dot(xlo, xl[h, :HD, :TOK], NN)
            inv = lax.rsqrt(jnp.sum(mixed * mixed, axis=0, keepdims=True) / HD + epsilon)
            nbuf[:, head_cols(h)] = (mixed * inv * gain_col()).T.astype(BF16)

    def gain_col():
        return jnp.sum(jnp.where(ri == ci, gain_ref[...], 0.0), axis=1, keepdims=True)

    half = HEADS * HD
    width = half // NB

    def columns(b):
        side = 1 - c if b < NB else c
        return pl.ds(pl.multiple_of(side * half + (b % NB) * width, width), width)

    def project(g, b):
        mine = slice(2 * HD * g, 2 * HD * (g + 1))
        return dot(nbuf[:, mine], w_ref[mine, columns(b)], NN)

    def project_pair(g):
        for b in range(2 * NB):
            acc[b] = project(g, b) if g == 0 else acc[b] + project(g, b)

    KEY.wait()
    gram_stage(0)
    pl.semaphore_wait(barrier, 7 + jnp.minimum(z, 1))

    @pl.when(z > 0)
    def _():
        pl.semaphore_signal(ready, inc=1, device_id=(s - 16, c), device_id_type=MESH)

    send_tail(0)
    for g in range(1, PAIRS):
        gram_stage(g)
        send_tail(g)
    VAL.wait()
    def send_early(st):
        @pl.when(c == 0)
        def _():
            send_tail(st)

    def send_late(st):
        @pl.when(c == 1)
        def _():
            send_tail(st)

    for st in range(PAIRS, STAGES):
        cross_stage(st)
        send_early(st)
    row_sum(0)
    send_late(4)
    row_sum(1)
    send_late(5)
    QUERY.wait()
    prepare(0)
    row_sum(2)
    send_late(6)
    row_sum(3)
    send_late(7)
    send_late(8)
    prepare(1)
    row_sum(4)
    plane_sum(0)
    plane_sum(1)
    row_sum(5)
    plane_sum(2)
    give_back(0)
    plane_sum(3)
    row_sum(6)
    give_back(1)
    prepare(2)
    row_sum(7)
    give_back(2)
    row_sum(8)
    plane_sum(4)
    prepare(3)
    give_back(3)
    plane_sum(5)
    plane_sum(6)
    give_back(4)
    first = solve((0, 1))
    next(first)
    next(first)
    give_back(5)
    plane_sum(7)
    plane_sum(8)
    next(first)
    next(first)
    give_back(6)
    for _ in first:
        pass
    second = solve((2, 3))
    next(second)
    give_back(7)
    give_back(8)
    for _ in second:
        pass
    GAIN.wait()
    WEIGHT.wait()
    finish(4, 5)
    project_pair(0)
    project_pair(1)
    finish(6)
    project_pair(2)
    finish(7, 8)

    def pcopy(b):
        return pltpu.make_async_remote_copy(
            acc.at[b], other.at[b], ps.at[0], pr.at[b],
            device_id=(s, 1 - c), device_id_type=MESH,
        )

    for b in range(0, NB, 2):
        for e in (b, b + 1):
            acc[e] = acc[e] + project(PAIRS - 1, e)
        for e in (b, b + 1):
            pcopy(e).start()
    for b in range(NB, 2 * NB):
        acc[b] = acc[b] + project(PAIRS - 1, b)
    for b in range(NB):
        pcopy(b).wait_recv()
        out_ref[:, b * width : (b + 1) * width] = (acc[NB + b] + other[b]).astype(BF16)

    for i, (stages, slots) in enumerate(((9, 4), (9, 3), (6, 3))):
        group = [st for st in range(STAGES) if kind(st) == i]
        wait_bytes(ybuf.at[pl.ds(0, stages), pl.ds(0, slots), rows(group[0])], sent.at[i])

        @pl.when(z < LAST)
        def _():
            wait_bytes(zs.at[pl.ds(group[0], len(group)), rows(group[0])], zsd.at[i])

    wait_bytes(other, ps.at[0])


def on_device(query_rows, key_rows, value_rows, doc_lengths, norm_gain, out_weight):
    half = HEADS * HD
    st = STAGES
    dma = pltpu.SemaphoreType.DMA
    anywhere = pl.BlockSpec(memory_space=pl.ANY)
    return pl.pallas_call(
        kernel,
        out_shape=pltpu.VMEM((TOK, half), BF16),
        in_specs=[anywhere] * 6,
        out_specs=pl.BlockSpec(memory_space=pltpu.VMEM),
        scratch_shapes=[
            pltpu.VMEM((TOK, half), BF16),
            pltpu.VMEM((TOK, half), BF16),
            pltpu.VMEM((TOK, half), BF16),
            pltpu.VMEM((half, 2 * half), BF16),
            pltpu.VMEM((1, HD), jnp.int32),
            pltpu.VMEM((1, HD), F32),
            pltpu.VMEM((st, 4, CH, HD), F32),
            pltpu.VMEM((st, 4, CH, HD), F32),
            pltpu.VMEM((st, 4, CH, HD), F32),
            pltpu.VMEM((st, CH, HD), F32),
            pltpu.VMEM((st, CH, HD), F32),
            pltpu.VMEM((st, 4, CH, HD), F32),
            pltpu.VMEM((st, 4, CH, HD), F32),
            pltpu.VMEM((HEADS, TOK, HD), F32),
            pltpu.VMEM((HEADS, TOK, TOK), F32),
            pltpu.VMEM((HEADS, 2 * HD, 4 * HD), BF16),
            pltpu.VMEM((HEADS, 2 * HD, 2 * TOK), BF16),
            pltpu.VMEM((HEADS, HD, TOK), BF16),
            pltpu.VMEM((HEADS, TOK, TOK), F32),
            pltpu.VMEM((HEADS, TOK, TOK), F32),
            pltpu.VMEM((TOK, half), BF16),
            pltpu.VMEM((2 * NB, TOK, half // NB), F32),
            pltpu.VMEM((NB, TOK, half // NB), F32),
            pltpu.VMEM((TOK, TOK), F32),
            pltpu.VMEM((40, HD), F32),
            pltpu.VMEM((TOK, HD), F32),
            pltpu.VMEM((1, TOK), F32),
            dma((6,)),
            dma((3,)), dma((st,)), dma((st,)),
            dma((3,)), dma((st,)), dma((st,)),
            dma((1,)), dma((NB,)),
            pltpu.SemaphoreType.REGULAR,
        ],
        compiler_params=pltpu.CompilerParams(collective_id=0, has_side_effects=True),
        name="mesa",
    )(
        query_rows, key_rows, value_rows,
        doc_lengths.reshape(1, -1), norm_gain.reshape(1, -1), out_weight,
    )


def solution(mesh):
    in_specs = (P("seq", "head"), P("seq", "head"), P("seq", "head"), P(), P(), P("head", None))
    return jax.shard_map(
        on_device, mesh=mesh, in_specs=in_specs, out_specs=P("seq", "head"), check_vma=False
    )
```

```python
import jax
import jax.numpy as jnp
from jax import lax
from jax.experimental import pallas as pl
from jax.experimental.pallas import tpu as pltpu
from jax.sharding import PartitionSpec as P

MESH = pl.DeviceIdType.MESH
F32 = jnp.float32
BF16 = jnp.bfloat16
HD = 128
TOK = 128
HEADS = 8
PAIRS = 4
ITERS = 4
CH = 64
CG = 40
CROSS = ((0, 1), (2, 3), (4, 5), (6,), (7,))
STAGES = PAIRS + len(CROSS)
LAST = 7
NB = 4
epsilon = 1e-06
damping = 1.0

WR, WZ, WC, WP, WE, WEC = 0, 4, 8, 12, 16, 32


def split2(a):
    hi = a.astype(BF16)
    return hi, (a - hi.astype(F32)).astype(BF16)


def dot(a, b, dims):
    return lax.dot_general(a, b, (dims, ((), ())), preferred_element_type=F32)


NN, NT, TN = ((1,), (0,)), ((1,), (1,)), ((0,), (0,))


def kernel(
    q_hbm, k_hbm, v_hbm, len_hbm, gain_hbm, w_hbm, out_ref,
    q_ref, k_ref, v_ref, w_ref, len_ref, gain_ref,
    tbuf, ybuf, rbuf, zs, zr, eo, ebuf, qs, scq, lhs, xl, vt, mf, mg, nbuf, acc, other,
    mask_ref, wts, tail_ref, car_ref,
    lsem, sent, yr, xr, zsd, zrv, er, ps, pr, ready,
):
    s = lax.axis_index("seq")
    c = lax.axis_index("head")
    y = lax.rem(s, 4)
    row = s - y
    x = lax.rem(s // 4, 4)
    col = s - 4 * x
    z = s // 16

    def at_y(d):
        return row + lax.rem(y + d, 4)

    def at_x(d):
        return col + 4 * lax.rem(x + d, 4)

    barrier = pltpu.get_barrier_semaphore()
    for d in (1, 2, 3):
        pl.semaphore_signal(barrier, inc=1, device_id=(at_y(d), c), device_id_type=MESH)
        pl.semaphore_signal(barrier, inc=1, device_id=(at_x(d), c), device_id_type=MESH)
    pl.semaphore_signal(barrier, inc=1, device_id=(s, 1 - c), device_id_type=MESH)

    @pl.when(z < LAST)
    def _():
        pl.semaphore_signal(barrier, inc=1, device_id=(s + 16, c), device_id_type=MESH)

    loads = [
        pltpu.make_async_copy(a, b, lsem.at[i])
        for i, (a, b) in enumerate(
            [
                (len_hbm, len_ref), (k_hbm, k_ref), (v_hbm, v_ref),
                (q_hbm, q_ref), (gain_hbm, gain_ref), (w_hbm, w_ref),
            ]
        )
    ]
    LEN, KEY, VAL, QUERY, GAIN, WEIGHT = loads
    for cp in loads:
        cp.start()

    @pl.when(z == 0)
    def _():
        zr[...] = jnp.zeros_like(zr)

    LEN.wait()
    lrow = len_ref[...].astype(F32)
    ri = lax.broadcasted_iota(jnp.int32, (TOK, TOK), 0)
    ci = lax.broadcasted_iota(jnp.int32, (TOK, TOK), 1)
    lcol = jnp.sum(jnp.where(ri == ci, lrow, 0.0), axis=1, keepdims=True)
    srow = jnp.sum(jnp.where(ri < ci, lcol, 0.0), axis=0, keepdims=True)
    scol = jnp.sum(jnp.where(ci < ri, lrow, 0.0), axis=1, keepdims=True)
    base = (s * TOK).astype(F32)
    rf, cf = ri.astype(F32), ci.astype(F32)
    doc_col = jnp.sum(jnp.where(srow <= base + rf, 1.0, 0.0), axis=1, keepdims=True)
    doc_row = jnp.sum(jnp.where(scol <= base + cf, 1.0, 0.0), axis=0, keepdims=True)
    ends = jnp.sum(jnp.where(scol <= cf * TOK + (TOK - 1.0), 1.0, 0.0), axis=0, keepdims=True)
    shard = lax.broadcasted_iota(jnp.int32, (1, TOK), 1)

    def end_of(i):
        return jnp.sum(jnp.where(shard == i, ends, 0.0), axis=1, keepdims=True)

    def put(k, flag):
        wts[k : k + 1, :] = jnp.broadcast_to(jnp.where(flag, 1.0, 0.0), (1, HD))

    here, before = end_of(s), end_of(s - 1)
    car_ref[...] = jnp.where(doc_row == before, 1.0, 0.0)
    tail_ref[...] = jnp.broadcast_to(jnp.where(doc_col == here, 1.0, 0.0), (TOK, HD))
    mask_ref[...] = jnp.where((doc_col == doc_row) & (ri <= ci), 1.0, 0.0)
    dy = [end_of(row + i) for i in range(4)]
    dx = [end_of(16 * z + 4 * i + 3) for i in range(4)]
    dprev, dplane = end_of(row - 1), end_of(16 * z - 1)
    for i in range(4):
        put(WR + i, dy[i] == dy[3])
        put(WZ + i, dx[i] == dx[3])
        put(WC + i, (dx[i] == dprev) & (jnp.full((1, 1), i, jnp.int32) < x))
    put(WP, (dplane == dprev) & (dplane > 0.0))
    for t in range(1, 4):
        for i in range(t):
            put(WE + 4 * t + i, dy[i] == dy[t - 1])
        put(WEC + t, dprev == dy[t - 1])

    def wt(k):
        return wts[k : k + 1, :]

    def head_cols(h):
        return pl.ds(pl.multiple_of(h * HD, HD), HD)

    def rows(st):
        return pl.ds(0, CG if st < PAIRS else 32 * len(CROSS[st - PAIRS]))

    def kind(st):
        return 0 if st < PAIRS else 1 if len(CROSS[st - PAIRS]) == 2 else 2

    def ycopy(st, d):
        r = rows(st)
        return pltpu.make_async_remote_copy(
            tbuf.at[st, lax.rem(y + d, 4), r], ybuf.at[st, y, r], sent.at[kind(st)], yr.at[st],
            device_id=(at_y(d), c), device_id_type=MESH,
        )

    def xcopy(st, d):
        r = rows(st)
        return pltpu.make_async_remote_copy(
            rbuf.at[st, x, r], rbuf.at[st, x, r], sent.at[kind(st)], xr.at[st],
            device_id=(at_x(d), c), device_id_type=MESH,
        )

    def zcopy(st):
        r = rows(st)
        return pltpu.make_async_remote_copy(
            zs.at[st, r], zr.at[st, r], zsd.at[kind(st)], zrv.at[st],
            device_id=(lax.rem(s + 16, 128), c), device_id_type=MESH,
        )

    def ecopy(st, d):
        r = rows(st)
        return pltpu.make_async_remote_copy(
            eo.at[st, lax.rem(y + d, 4), r], ebuf.at[st, y, r], sent.at[kind(st)], er.at[st],
            device_id=(at_y(d), c), device_id_type=MESH,
        )

    def wait_bytes(ref, sem):
        pltpu.make_async_copy(ref, ref, sem).wait()

    def arrived(ref, sem, st):
        wait_bytes(ref.at[st, pl.ds(0, 3), rows(st)], sem.at[st])

    def send_tail(st):
        r = rows(st)
        for d in (2, 1, 3):
            ycopy(st, d).start()
        ybuf[st, y, r] = tbuf[st, y, r]

    lane = lax.broadcasted_iota(jnp.int32, (32, HD), 1)

    def gram_stage(g):
        grams = []
        for h in (2 * g, 2 * g + 1):
            k = k_ref[:, head_cols(h)]
            kf = k.astype(F32)
            ks = lax.rsqrt(jnp.sum(kf * kf, axis=1, keepdims=True) + epsilon)
            hi, lo = split2(kf * (ks * ks) * tail_ref[...])
            grams.append(dot(jnp.concatenate([hi, lo], 0), jnp.concatenate([k, k], 0), TN))
        blocks = []
        for gram in grams:
            blocks.append(gram[:32])
            blocks.append(jnp.where(lane < 32, pltpu.roll(gram[96:], 32, 1), gram[32:64]))
        blocks.append(jnp.where(lane < 64, pltpu.roll(grams[1][64:96], 64, 1), grams[0][64:96]))
        packed = jnp.concatenate(blocks, 0)
        for o in range(4):
            tbuf[g, o, :CG] = packed[CG * o : CG * (o + 1)]

    def gram_of(g, i):
        packed = jnp.concatenate([ebuf[g, o, :CG] for o in range(4)], 0)
        first, second, third = packed[64 * i : 64 * i + 32], packed[64 * i + 32 : 64 * i + 64], packed[128:]
        if i == 1:
            third = pltpu.roll(third, 64, 1)
        upper = jnp.concatenate([first, second, third, pltpu.roll(second, 96, 1)], 0)
        return jnp.where(ci // 32 >= ri // 32, upper, upper.T)

    def cross_stage(st):
        parts = []
        for h in CROSS[st - PAIRS]:
            k = k_ref[:, head_cols(h)]
            v = v_ref[:, head_cols(h)]
            kf = k.astype(F32)
            ks = lax.rsqrt(jnp.sum(kf * kf, axis=1, keepdims=True) + epsilon)
            hi, lo = split2(kf * ks * tail_ref[...])
            parts.append(dot(jnp.concatenate([v, v], 0), jnp.concatenate([hi, lo], 0), TN))
        n = 32 * len(parts)
        stacked = jnp.concatenate(parts, 0)
        for o in range(4):
            tbuf[st, o, :n] = stacked[n * o : n * (o + 1)]

    def row_sum(st):
        r = rows(st)
        arrived(ybuf, yr, st)
        total = ybuf[st, 3, r]
        for i in range(3):
            total = total + wt(WR + i) * ybuf[st, i, r]
        rbuf[st, x, r] = total
        for d in (2, 1, 3):
            xcopy(st, d).start()

    def plane_sum(st):
        r = rows(st)
        arrived(rbuf, xr, st)
        total = rbuf[st, 3, r]
        for i in range(3):
            total = total + wt(WZ + i) * rbuf[st, i, r]
        zs[st, r] = total

        @pl.when(z < LAST)
        def _():
            if st == 0:
                pl.semaphore_wait(ready, 1)
            zcopy(st).start()

    def give_back(st):
        r = rows(st)

        @pl.when(z > 0)
        def _():
            zcopy(st).wait_recv()

        come = wt(WP) * zr[st, r]
        for i in range(3):
            come = come + wt(WC + i) * rbuf[st, i, r]
        eo[st, 0, r] = come
        parts = [ybuf[st, i, r] for i in range(3)]
        for t in range(1, 4):
            total = wt(WEC + t) * come
            for i in range(t):
                total = total + wt(WE + 4 * t + i) * parts[i]
            eo[st, t, r] = total
        for d in (2, 1, 3):
            ecopy(st, d).start()
        ebuf[st, y, r] = eo[st, y, r]

    def prepare(g):
        for h in (2 * g, 2 * g + 1):
            q = q_ref[:, head_cols(h)].astype(F32).T
            q = q * lax.rsqrt(jnp.sum(q * q, axis=0, keepdims=True) + epsilon)
            k = k_ref[:, head_cols(h)]
            kf = k.astype(F32)
            ks = lax.rsqrt(jnp.sum(kf * kf, axis=1, keepdims=True) + epsilon)
            m = mask_ref[...] * ks
            mf[h] = m
            mg[h] = m * ks
            hi, lo = split2(q)
            qs[h] = q
            scq[h] = dot(jnp.concatenate([k, k], 1), jnp.concatenate([hi, lo], 0), NN)
            khi, klo = split2(dot(k, k, NT))
            lhs[h, :HD, HD : 2 * HD] = kf.T.astype(BF16)
            lhs[h, HD:, HD : 2 * HD] = khi
            lhs[h, :HD, 3 * HD :] = jnp.zeros_like(klo)
            lhs[h, HD:, 3 * HD :] = klo
            vt[h] = v_ref[:, head_cols(h)].astype(F32).T.astype(BF16)

    def columns_of(vector, scores):
        hi, lo = split2(vector)
        shi, slo = split2(scores)
        car16 = car_ref[...].astype(BF16)
        return jnp.concatenate([hi * car16, shi], 0), jnp.concatenate([lo * car16, slo], 0)

    def solve(pairs):
        state = []
        for g, i in [(g, i) for g in pairs for i in range(2)]:
            if i == 0:
                arrived(ebuf, er, g)
            h = 2 * g + i
            k = k_ref[:, head_cols(h)]
            ghi, glo = split2(gram_of(g, i))
            shi, slo = split2(dot(jnp.concatenate([k, k], 1), jnp.concatenate([ghi, glo], 0), NN))
            lhs[h, :HD, :HD] = ghi
            lhs[h, HD:, :HD] = shi
            lhs[h, :HD, 2 * HD : 3 * HD] = glo
            lhs[h, HD:, 2 * HD : 3 * HD] = slo
            q, sc = qs[h], scq[h]
            n = jnp.sum(q * q, axis=0, keepdims=True)
            state.append(dict(h=h, p=q, sp=sc, r=q, sr=sc, n=n))
            if i == 1:
                yield
        for it in range(ITERS):
            last = it == ITERS - 1
            rows_here = HD if last else 2 * HD
            for e in state:
                p, sp, h = e["p"], e["sp"], e["h"]
                hi, lo = columns_of(p, sp * mg[h])
                both = dot(lhs[h, :rows_here, : 2 * HD], jnp.concatenate([hi, lo], 1), NN)
                both = both[:, :TOK] + both[:, TOK:] + dot(lhs[h, :rows_here, 2 * HD :], hi, NN)
                a = both[:HD] + damping * p
                alpha = e["n"] / (jnp.sum(p * a, axis=0, keepdims=True) + epsilon)
                e["x"] = alpha * p if it == 0 else e["x"] + alpha * p
                e["sx"] = alpha * sp if it == 0 else e["sx"] + alpha * sp
                if not last:
                    sa = both[HD:] + damping * sp
                    e["r"] = e["r"] - alpha * a
                    e["sr"] = e["sr"] - alpha * sa
                    new = jnp.sum(e["r"] * e["r"], axis=0, keepdims=True)
                    beta = new / (e["n"] + epsilon)
                    e["p"] = e["r"] + beta * p
                    e["sp"] = e["sr"] + beta * sp
                    e["n"] = new
            yield
        for e in state:
            h = e["h"]
            hi, lo = columns_of(e["x"], e["sx"] * mf[h])
            xl[h] = jnp.concatenate([hi, lo], 1)

    def finish(*stages):
        for st in stages:
            arrived(ebuf, er, st)
        states = []
        for st in stages:
            n = 32 * len(CROSS[st - PAIRS])
            stacked = jnp.concatenate([ebuf[st, o, :n] for o in range(4)], 0)
            for i, h in enumerate(CROSS[st - PAIRS]):
                states.append((h, stacked[HD * i : HD * (i + 1)]))
        for h, cross in states:
            xhi, xlo = split2(cross)
            mixed = dot(jnp.concatenate([xhi, vt[h]], 1), xl[h], NN)
            mixed = mixed[:, :TOK] + mixed[:, TOK:] + dot(xlo, xl[h, :HD, :TOK], NN)
            inv = lax.rsqrt(jnp.sum(mixed * mixed, axis=0, keepdims=True) / HD + epsilon)
            nbuf[:, head_cols(h)] = (mixed * inv * gain_col()).T.astype(BF16)

    def gain_col():
        return jnp.sum(jnp.where(ri == ci, gain_ref[...], 0.0), axis=1, keepdims=True)

    half = HEADS * HD
    width = half // NB

    def columns(b):
        side = 1 - c if b < NB else c
        return pl.ds(pl.multiple_of(side * half + (b % NB) * width, width), width)

    def project(g, b):
        mine = slice(2 * HD * g, 2 * HD * (g + 1))
        return dot(nbuf[:, mine], w_ref[mine, columns(b)], NN)

    def project_pair(g):
        for b in range(2 * NB):
            acc[b] = project(g, b) if g == 0 else acc[b] + project(g, b)

    KEY.wait()
    gram_stage(0)
    pl.semaphore_wait(barrier, 7 + jnp.minimum(z, 1))

    @pl.when(z > 0)
    def _():
        pl.semaphore_signal(ready, inc=1, device_id=(s - 16, c), device_id_type=MESH)

    def send_early(st):
        @pl.when(c == 0)
        def _():
            send_tail(st)

    def send_late(st):
        @pl.when(c == 1)
        def _():
            send_tail(st)

    send_tail(0)
    for g in range(1, PAIRS):
        gram_stage(g)
        send_early(g)
        if g > 1:
            send_late(g - 1)
    VAL.wait()
    for st in range(PAIRS, STAGES):
        cross_stage(st)
        send_early(st)
        if st == PAIRS:
            send_late(PAIRS - 1)
    row_sum(0)
    row_sum(1)
    send_late(4)
    QUERY.wait()
    prepare(0)
    row_sum(2)
    send_late(5)
    row_sum(3)
    send_late(6)
    prepare(1)
    send_late(7)
    send_late(8)
    row_sum(4)
    plane_sum(0)
    plane_sum(1)
    row_sum(5)
    plane_sum(2)
    give_back(0)
    plane_sum(3)
    row_sum(6)
    give_back(1)
    prepare(2)
    row_sum(7)
    row_sum(8)
    plane_sum(4)
    give_back(2)
    prepare(3)
    plane_sum(5)
    give_back(3)
    first = solve((0, 1))
    next(first)
    plane_sum(6)
    give_back(4)
    next(first)
    next(first)
    give_back(5)
    plane_sum(7)
    plane_sum(8)
    next(first)
    next(first)
    give_back(6)
    for _ in first:
        pass
    second = solve((2, 3))
    next(second)
    next(second)
    give_back(7)
    give_back(8)
    for _ in second:
        pass
    GAIN.wait()
    WEIGHT.wait()
    finish(4, 5)
    project_pair(0)
    project_pair(1)
    finish(6)
    project_pair(2)
    finish(7, 8)

    def pcopy(b):
        return pltpu.make_async_remote_copy(
            acc.at[b], other.at[b], ps.at[0], pr.at[b],
            device_id=(s, 1 - c), device_id_type=MESH,
        )

    for b in range(0, NB, 2):
        for e in (b, b + 1):
            acc[e] = acc[e] + project(PAIRS - 1, e)
        for e in (b, b + 1):
            pcopy(e).start()
    for b in range(NB, 2 * NB):
        acc[b] = acc[b] + project(PAIRS - 1, b)
    for b in range(NB):
        pcopy(b).wait_recv()
        out_ref[:, b * width : (b + 1) * width] = (acc[NB + b] + other[b]).astype(BF16)

    for i, (stages, slots) in enumerate(((9, 4), (9, 3), (6, 3))):
        group = [st for st in range(STAGES) if kind(st) == i]
        wait_bytes(ybuf.at[pl.ds(0, stages), pl.ds(0, slots), rows(group[0])], sent.at[i])

        @pl.when(z < LAST)
        def _():
            wait_bytes(zs.at[pl.ds(group[0], len(group)), rows(group[0])], zsd.at[i])

    wait_bytes(other, ps.at[0])


def on_device(query_rows, key_rows, value_rows, doc_lengths, norm_gain, out_weight):
    half = HEADS * HD
    st = STAGES
    dma = pltpu.SemaphoreType.DMA
    anywhere = pl.BlockSpec(memory_space=pl.ANY)
    return pl.pallas_call(
        kernel,
        out_shape=pltpu.VMEM((TOK, half), BF16),
        in_specs=[anywhere] * 6,
        out_specs=pl.BlockSpec(memory_space=pltpu.VMEM),
        scratch_shapes=[
            pltpu.VMEM((TOK, half), BF16),
            pltpu.VMEM((TOK, half), BF16),
            pltpu.VMEM((TOK, half), BF16),
            pltpu.VMEM((half, 2 * half), BF16),
            pltpu.VMEM((1, HD), jnp.int32),
            pltpu.VMEM((1, HD), F32),
            pltpu.VMEM((st, 4, CH, HD), F32),
            pltpu.VMEM((st, 4, CH, HD), F32),
            pltpu.VMEM((st, 4, CH, HD), F32),
            pltpu.VMEM((st, CH, HD), F32),
            pltpu.VMEM((st, CH, HD), F32),
            pltpu.VMEM((st, 4, CH, HD), F32),
            pltpu.VMEM((st, 4, CH, HD), F32),
            pltpu.VMEM((HEADS, TOK, HD), F32),
            pltpu.VMEM((HEADS, TOK, TOK), F32),
            pltpu.VMEM((HEADS, 2 * HD, 4 * HD), BF16),
            pltpu.VMEM((HEADS, 2 * HD, 2 * TOK), BF16),
            pltpu.VMEM((HEADS, HD, TOK), BF16),
            pltpu.VMEM((HEADS, TOK, TOK), F32),
            pltpu.VMEM((HEADS, TOK, TOK), F32),
            pltpu.VMEM((TOK, half), BF16),
            pltpu.VMEM((2 * NB, TOK, half // NB), F32),
            pltpu.VMEM((NB, TOK, half // NB), F32),
            pltpu.VMEM((TOK, TOK), F32),
            pltpu.VMEM((40, HD), F32),
            pltpu.VMEM((TOK, HD), F32),
            pltpu.VMEM((1, TOK), F32),
            dma((6,)),
            dma((3,)), dma((st,)), dma((st,)),
            dma((3,)), dma((st,)), dma((st,)),
            dma((1,)), dma((NB,)),
            pltpu.SemaphoreType.REGULAR,
        ],
        compiler_params=pltpu.CompilerParams(collective_id=0, has_side_effects=True),
        name="mesa",
    )(
        query_rows, key_rows, value_rows,
        doc_lengths.reshape(1, -1), norm_gain.reshape(1, -1), out_weight,
    )


def solution(mesh):
    in_specs = (P("seq", "head"), P("seq", "head"), P("seq", "head"), P(), P(), P("head", None))
    return jax.shard_map(
        on_device, mesh=mesh, in_specs=in_specs, out_specs=P("seq", "head"), check_vma=False
    )
```

```python
import jax
import jax.numpy as jnp
from jax import lax
from jax.experimental import pallas as pl
from jax.experimental.pallas import tpu as pltpu
from jax.sharding import PartitionSpec as P

MESH = pl.DeviceIdType.MESH
F32 = jnp.float32
BF16 = jnp.bfloat16
HD = 128
TOK = 128
HEADS = 8
PAIRS = 4
ITERS = 4
CH = 64
CG = 40
CROSS = ((0, 1), (2, 3), (4, 5), (6,), (7,))
STAGES = PAIRS + len(CROSS)
LAST = 7
TURN = 4
NB = 4
epsilon = 1e-06
damping = 1.0

WR, WZ, WC, WP, WE, WEC = 0, 4, 8, 12, 16, 32


def split2(a):
    hi = a.astype(BF16)
    return hi, (a - hi.astype(F32)).astype(BF16)


def dot(a, b, dims):
    return lax.dot_general(a, b, (dims, ((), ())), preferred_element_type=F32)


NN, NT, TN = ((1,), (0,)), ((1,), (1,)), ((0,), (0,))


def kernel(
    q_hbm, k_hbm, v_hbm, len_hbm, gain_hbm, w_hbm, out_ref,
    q_ref, k_ref, v_ref, w_ref, len_ref, gain_ref,
    tbuf, ybuf, rbuf, zs, zr, eo, ebuf, qs, scq, lhs, xl, vt, mf, mg, nbuf, acc, other,
    mask_ref, wts, tail_ref, car_ref,
    lsem, sent, yr, xr, zsd, zrv, er, ps, pr, ready,
):
    s = lax.axis_index("seq")
    c = lax.axis_index("head")
    y = lax.rem(s, 4)
    row = s - y
    x = lax.rem(s // 4, 4)
    col = s - 4 * x
    z = s // 16

    def at_y(d):
        return row + lax.rem(y + d, 4)

    def at_x(d):
        return col + 4 * lax.rem(x + d, 4)

    barrier = pltpu.get_barrier_semaphore()
    for d in (1, 2, 3):
        pl.semaphore_signal(barrier, inc=1, device_id=(at_y(d), c), device_id_type=MESH)
        pl.semaphore_signal(barrier, inc=1, device_id=(at_x(d), c), device_id_type=MESH)
    pl.semaphore_signal(barrier, inc=1, device_id=(s, 1 - c), device_id_type=MESH)

    @pl.when(z < TURN)
    def _():
        pl.semaphore_signal(
            barrier, inc=1, device_id=(lax.rem(s + 16, 128), c), device_id_type=MESH
        )

    @pl.when(z > TURN)
    def _():
        pl.semaphore_signal(
            barrier, inc=1, device_id=(lax.rem(s + 112, 128), c), device_id_type=MESH
        )

    loads = [
        pltpu.make_async_copy(a, b, lsem.at[i])
        for i, (a, b) in enumerate(
            [
                (len_hbm, len_ref), (k_hbm, k_ref), (v_hbm, v_ref),
                (q_hbm, q_ref), (gain_hbm, gain_ref), (w_hbm, w_ref),
            ]
        )
    ]
    LEN, KEY, VAL, QUERY, GAIN, WEIGHT = loads
    for cp in loads:
        cp.start()

    @pl.when(z == 0)
    def _():
        zr[...] = jnp.zeros_like(zr)

    LEN.wait()
    lrow = len_ref[...].astype(F32)
    ri = lax.broadcasted_iota(jnp.int32, (TOK, TOK), 0)
    ci = lax.broadcasted_iota(jnp.int32, (TOK, TOK), 1)
    lcol = jnp.sum(jnp.where(ri == ci, lrow, 0.0), axis=1, keepdims=True)
    srow = jnp.sum(jnp.where(ri < ci, lcol, 0.0), axis=0, keepdims=True)
    scol = jnp.sum(jnp.where(ci < ri, lrow, 0.0), axis=1, keepdims=True)
    base = (s * TOK).astype(F32)
    rf, cf = ri.astype(F32), ci.astype(F32)
    doc_col = jnp.sum(jnp.where(srow <= base + rf, 1.0, 0.0), axis=1, keepdims=True)
    doc_row = jnp.sum(jnp.where(scol <= base + cf, 1.0, 0.0), axis=0, keepdims=True)
    ends = jnp.sum(jnp.where(scol <= cf * TOK + (TOK - 1.0), 1.0, 0.0), axis=0, keepdims=True)
    shard = lax.broadcasted_iota(jnp.int32, (1, TOK), 1)

    def end_of(i):
        return jnp.sum(jnp.where(shard == i, ends, 0.0), axis=1, keepdims=True)

    def put(k, flag):
        wts[k : k + 1, :] = jnp.broadcast_to(jnp.where(flag, 1.0, 0.0), (1, HD))

    here, before = end_of(s), end_of(s - 1)
    car_ref[...] = jnp.where(doc_row == before, 1.0, 0.0)
    tail_ref[...] = jnp.broadcast_to(jnp.where(doc_col == here, 1.0, 0.0), (TOK, HD))
    mask_ref[...] = jnp.where((doc_col == doc_row) & (ri <= ci), 1.0, 0.0)
    dy = [end_of(row + i) for i in range(4)]
    dx = [end_of(16 * z + 4 * i + 3) for i in range(4)]
    dprev, dplane = end_of(row - 1), end_of(16 * z - 1)
    for i in range(4):
        put(WR + i, dy[i] == dy[3])
        put(WZ + i, dx[i] == dx[3])
        put(WC + i, (dx[i] == dprev) & (jnp.full((1, 1), i, jnp.int32) < x))
    put(WP, (dplane == dprev) & (dplane > 0.0))
    for t in range(1, 4):
        for i in range(t):
            put(WE + 4 * t + i, dy[i] == dy[t - 1])
        put(WEC + t, dprev == dy[t - 1])

    def wt(k):
        return wts[k : k + 1, :]

    def head_cols(h):
        return pl.ds(pl.multiple_of(h * HD, HD), HD)

    def rows(st):
        return pl.ds(0, CG if st < PAIRS else 32 * len(CROSS[st - PAIRS]))

    def kind(st):
        return 0 if st < PAIRS else 1 if len(CROSS[st - PAIRS]) == 2 else 2

    def ycopy(st, d):
        r = rows(st)
        return pltpu.make_async_remote_copy(
            tbuf.at[st, lax.rem(y + d, 4), r], ybuf.at[st, y, r], sent.at[kind(st)], yr.at[st],
            device_id=(at_y(d), c), device_id_type=MESH,
        )

    def xcopy(st, d):
        r = rows(st)
        return pltpu.make_async_remote_copy(
            rbuf.at[st, x, r], rbuf.at[st, x, r], sent.at[kind(st)], xr.at[st],
            device_id=(at_x(d), c), device_id_type=MESH,
        )

    def zcopy(st):
        r = rows(st)
        return pltpu.make_async_remote_copy(
            zs.at[st, r], zr.at[st, r], zsd.at[kind(st)], zrv.at[st],
            device_id=(lax.rem(s + 16, 128), c), device_id_type=MESH,
        )

    def ecopy(st, d):
        r = rows(st)
        return pltpu.make_async_remote_copy(
            eo.at[st, lax.rem(y + d, 4), r], ebuf.at[st, y, r], sent.at[kind(st)], er.at[st],
            device_id=(at_y(d), c), device_id_type=MESH,
        )

    def wait_bytes(ref, sem):
        pltpu.make_async_copy(ref, ref, sem).wait()

    def arrived(ref, sem, st):
        wait_bytes(ref.at[st, pl.ds(0, 3), rows(st)], sem.at[st])

    def send_tail(st):
        r = rows(st)
        for d in (2, 1, 3):
            ycopy(st, d).start()
        ybuf[st, y, r] = tbuf[st, y, r]

    lane = lax.broadcasted_iota(jnp.int32, (32, HD), 1)

    def gram_stage(g):
        grams = []
        for h in (2 * g, 2 * g + 1):
            k = k_ref[:, head_cols(h)]
            kf = k.astype(F32)
            ks = lax.rsqrt(jnp.sum(kf * kf, axis=1, keepdims=True) + epsilon)
            hi, lo = split2(kf * (ks * ks) * tail_ref[...])
            grams.append(dot(jnp.concatenate([hi, lo], 0), jnp.concatenate([k, k], 0), TN))
        blocks = []
        for gram in grams:
            blocks.append(gram[:32])
            blocks.append(jnp.where(lane < 32, pltpu.roll(gram[96:], 32, 1), gram[32:64]))
        blocks.append(jnp.where(lane < 64, pltpu.roll(grams[1][64:96], 64, 1), grams[0][64:96]))
        packed = jnp.concatenate(blocks, 0)
        for o in range(4):
            tbuf[g, o, :CG] = packed[CG * o : CG * (o + 1)]

    def gram_of(g, i):
        packed = jnp.concatenate([ebuf[g, o, :CG] for o in range(4)], 0)
        first, second, third = packed[64 * i : 64 * i + 32], packed[64 * i + 32 : 64 * i + 64], packed[128:]
        if i == 1:
            third = pltpu.roll(third, 64, 1)
        upper = jnp.concatenate([first, second, third, pltpu.roll(second, 96, 1)], 0)
        return jnp.where(ci // 32 >= ri // 32, upper, upper.T)

    def cross_stage(st):
        parts = []
        for h in CROSS[st - PAIRS]:
            k = k_ref[:, head_cols(h)]
            v = v_ref[:, head_cols(h)]
            kf = k.astype(F32)
            ks = lax.rsqrt(jnp.sum(kf * kf, axis=1, keepdims=True) + epsilon)
            hi, lo = split2(kf * ks * tail_ref[...])
            parts.append(dot(jnp.concatenate([v, v], 0), jnp.concatenate([hi, lo], 0), TN))
        n = 32 * len(parts)
        stacked = jnp.concatenate(parts, 0)
        for o in range(4):
            tbuf[st, o, :n] = stacked[n * o : n * (o + 1)]

    def row_sum(st):
        r = rows(st)
        arrived(ybuf, yr, st)
        total = ybuf[st, 3, r]
        for i in range(3):
            total = total + wt(WR + i) * ybuf[st, i, r]
        rbuf[st, x, r] = total
        for d in (2, 1, 3):
            xcopy(st, d).start()

    def plane_sum(st):
        r = rows(st)
        arrived(rbuf, xr, st)
        total = rbuf[st, 3, r]
        for i in range(3):
            total = total + wt(WZ + i) * rbuf[st, i, r]
        zs[st, r] = total

        if st == 0:

            @pl.when(z < TURN)
            def _():
                pl.semaphore_wait(ready, 1)

        @pl.when(z < LAST)
        def _():
            zcopy(st).start()

    def give_back(st):
        r = rows(st)

        @pl.when(z > 0)
        def _():
            zcopy(st).wait_recv()

        come = wt(WP) * zr[st, r]
        for i in range(3):
            come = come + wt(WC + i) * rbuf[st, i, r]
        eo[st, 0, r] = come
        parts = [ybuf[st, i, r] for i in range(3)]
        for t in range(1, 4):
            total = wt(WEC + t) * come
            for i in range(t):
                total = total + wt(WE + 4 * t + i) * parts[i]
            eo[st, t, r] = total
        for d in (2, 1, 3):
            ecopy(st, d).start()
        ebuf[st, y, r] = eo[st, y, r]

    def prepare(g):
        for h in (2 * g, 2 * g + 1):
            q = q_ref[:, head_cols(h)].astype(F32).T
            q = q * lax.rsqrt(jnp.sum(q * q, axis=0, keepdims=True) + epsilon)
            k = k_ref[:, head_cols(h)]
            kf = k.astype(F32)
            ks = lax.rsqrt(jnp.sum(kf * kf, axis=1, keepdims=True) + epsilon)
            m = mask_ref[...] * ks
            mf[h] = m
            mg[h] = m * ks
            hi, lo = split2(q)
            qs[h] = q
            scq[h] = dot(jnp.concatenate([k, k], 1), jnp.concatenate([hi, lo], 0), NN)
            khi, klo = split2(dot(k, k, NT))
            lhs[h, :HD, HD : 2 * HD] = kf.T.astype(BF16)
            lhs[h, HD:, HD : 2 * HD] = khi
            lhs[h, :HD, 3 * HD :] = jnp.zeros_like(klo)
            lhs[h, HD:, 3 * HD :] = klo
            vt[h] = v_ref[:, head_cols(h)].astype(F32).T.astype(BF16)

    def columns_of(vector, scores):
        hi, lo = split2(vector)
        shi, slo = split2(scores)
        car16 = car_ref[...].astype(BF16)
        return jnp.concatenate([hi * car16, shi], 0), jnp.concatenate([lo * car16, slo], 0)

    def solve(pairs):
        state = []
        for g, i in [(g, i) for g in pairs for i in range(2)]:
            if i == 0:
                arrived(ebuf, er, g)
            h = 2 * g + i
            k = k_ref[:, head_cols(h)]
            ghi, glo = split2(gram_of(g, i))
            shi, slo = split2(dot(jnp.concatenate([k, k], 1), jnp.concatenate([ghi, glo], 0), NN))
            lhs[h, :HD, :HD] = ghi
            lhs[h, HD:, :HD] = shi
            lhs[h, :HD, 2 * HD : 3 * HD] = glo
            lhs[h, HD:, 2 * HD : 3 * HD] = slo
            q, sc = qs[h], scq[h]
            n = jnp.sum(q * q, axis=0, keepdims=True)
            state.append(dict(h=h, p=q, sp=sc, r=q, sr=sc, n=n))
            if i == 1:
                yield
        for it in range(ITERS):
            last = it == ITERS - 1
            rows_here = HD if last else 2 * HD
            for e in state:
                p, sp, h = e["p"], e["sp"], e["h"]
                hi, lo = columns_of(p, sp * mg[h])
                both = dot(lhs[h, :rows_here, : 2 * HD], jnp.concatenate([hi, lo], 1), NN)
                both = both[:, :TOK] + both[:, TOK:] + dot(lhs[h, :rows_here, 2 * HD :], hi, NN)
                a = both[:HD] + damping * p
                alpha = e["n"] / (jnp.sum(p * a, axis=0, keepdims=True) + epsilon)
                e["x"] = alpha * p if it == 0 else e["x"] + alpha * p
                e["sx"] = alpha * sp if it == 0 else e["sx"] + alpha * sp
                if not last:
                    sa = both[HD:] + damping * sp
                    e["r"] = e["r"] - alpha * a
                    e["sr"] = e["sr"] - alpha * sa
                    new = jnp.sum(e["r"] * e["r"], axis=0, keepdims=True)
                    beta = new / (e["n"] + epsilon)
                    e["p"] = e["r"] + beta * p
                    e["sp"] = e["sr"] + beta * sp
                    e["n"] = new
            yield
        for e in state:
            h = e["h"]
            hi, lo = columns_of(e["x"], e["sx"] * mf[h])
            xl[h] = jnp.concatenate([hi, lo], 1)

    def finish(*stages):
        for st in stages:
            arrived(ebuf, er, st)
        states = []
        for st in stages:
            n = 32 * len(CROSS[st - PAIRS])
            stacked = jnp.concatenate([ebuf[st, o, :n] for o in range(4)], 0)
            for i, h in enumerate(CROSS[st - PAIRS]):
                states.append((h, stacked[HD * i : HD * (i + 1)]))
        for h, cross in states:
            xhi, xlo = split2(cross)
            mixed = dot(jnp.concatenate([xhi, vt[h]], 1), xl[h], NN)
            mixed = mixed[:, :TOK] + mixed[:, TOK:] + dot(xlo, xl[h, :HD, :TOK], NN)
            inv = lax.rsqrt(jnp.sum(mixed * mixed, axis=0, keepdims=True) / HD + epsilon)
            nbuf[:, head_cols(h)] = (mixed * inv * gain_col()).T.astype(BF16)

    def gain_col():
        return jnp.sum(jnp.where(ri == ci, gain_ref[...], 0.0), axis=1, keepdims=True)

    half = HEADS * HD
    width = half // NB

    def columns(b):
        side = 1 - c if b < NB else c
        return pl.ds(pl.multiple_of(side * half + (b % NB) * width, width), width)

    def project(g, b):
        mine = slice(2 * HD * g, 2 * HD * (g + 1))
        return dot(nbuf[:, mine], w_ref[mine, columns(b)], NN)

    def project_pair(g):
        for b in range(2 * NB):
            acc[b] = project(g, b) if g == 0 else acc[b] + project(g, b)

    KEY.wait()
    gram_stage(0)
    greeted = jnp.where((z > 0) & (z <= TURN), 1, 0) + jnp.where((z >= TURN) & (z < LAST), 1, 0)
    pl.semaphore_wait(barrier, 7 + greeted)

    @pl.when((z > 0) & (z <= TURN))
    def _():
        pl.semaphore_signal(
            ready, inc=1, device_id=(lax.rem(s + 112, 128), c), device_id_type=MESH
        )

    def send_early(st):
        @pl.when(c == 0)
        def _():
            send_tail(st)

    def send_late(st):
        @pl.when(c == 1)
        def _():
            send_tail(st)

    send_tail(0)
    for g in range(1, PAIRS):
        gram_stage(g)
        send_tail(g)
    VAL.wait()
    for st in range(PAIRS, STAGES):
        cross_stage(st)
        send_early(st)
    row_sum(0)
    send_late(4)
    row_sum(1)
    send_late(5)
    QUERY.wait()
    prepare(0)
    row_sum(2)
    send_late(6)
    row_sum(3)
    send_late(7)
    send_late(8)
    prepare(1)
    row_sum(4)
    plane_sum(0)
    plane_sum(1)
    row_sum(5)
    plane_sum(2)
    give_back(0)
    plane_sum(3)
    row_sum(6)
    give_back(1)
    prepare(2)
    row_sum(7)
    row_sum(8)
    plane_sum(4)
    give_back(2)
    prepare(3)
    plane_sum(5)
    give_back(3)
    first = solve((0, 1))
    next(first)
    plane_sum(6)
    give_back(4)
    next(first)
    next(first)
    give_back(5)
    plane_sum(7)
    plane_sum(8)
    next(first)
    next(first)
    give_back(6)
    for _ in first:
        pass
    second = solve((2, 3))
    next(second)
    next(second)
    give_back(7)
    give_back(8)
    for _ in second:
        pass
    GAIN.wait()
    WEIGHT.wait()
    finish(4, 5)
    project_pair(0)
    project_pair(1)
    finish(6)
    project_pair(2)
    finish(7, 8)

    def pcopy(b):
        return pltpu.make_async_remote_copy(
            acc.at[b], other.at[b], ps.at[0], pr.at[b],
            device_id=(s, 1 - c), device_id_type=MESH,
        )

    for b in range(0, NB, 2):
        for e in (b, b + 1):
            acc[e] = acc[e] + project(PAIRS - 1, e)
        for e in (b, b + 1):
            pcopy(e).start()
    for b in range(NB, 2 * NB):
        acc[b] = acc[b] + project(PAIRS - 1, b)
    for b in range(NB):
        pcopy(b).wait_recv()
        out_ref[:, b * width : (b + 1) * width] = (acc[NB + b] + other[b]).astype(BF16)

    for i, (stages, slots) in enumerate(((9, 4), (9, 3), (6, 3))):
        group = [st for st in range(STAGES) if kind(st) == i]
        wait_bytes(ybuf.at[pl.ds(0, stages), pl.ds(0, slots), rows(group[0])], sent.at[i])

        @pl.when(z < LAST)
        def _():
            wait_bytes(zs.at[pl.ds(group[0], len(group)), rows(group[0])], zsd.at[i])

    wait_bytes(other, ps.at[0])


def on_device(query_rows, key_rows, value_rows, doc_lengths, norm_gain, out_weight):
    half = HEADS * HD
    st = STAGES
    dma = pltpu.SemaphoreType.DMA
    anywhere = pl.BlockSpec(memory_space=pl.ANY)
    return pl.pallas_call(
        kernel,
        out_shape=pltpu.VMEM((TOK, half), BF16),
        in_specs=[anywhere] * 6,
        out_specs=pl.BlockSpec(memory_space=pltpu.VMEM),
        scratch_shapes=[
            pltpu.VMEM((TOK, half), BF16),
            pltpu.VMEM((TOK, half), BF16),
            pltpu.VMEM((TOK, half), BF16),
            pltpu.VMEM((half, 2 * half), BF16),
            pltpu.VMEM((1, HD), jnp.int32),
            pltpu.VMEM((1, HD), F32),
            pltpu.VMEM((st, 4, CH, HD), F32),
            pltpu.VMEM((st, 4, CH, HD), F32),
            pltpu.VMEM((st, 4, CH, HD), F32),
            pltpu.VMEM((st, CH, HD), F32),
            pltpu.VMEM((st, CH, HD), F32),
            pltpu.VMEM((st, 4, CH, HD), F32),
            pltpu.VMEM((st, 4, CH, HD), F32),
            pltpu.VMEM((HEADS, TOK, HD), F32),
            pltpu.VMEM((HEADS, TOK, TOK), F32),
            pltpu.VMEM((HEADS, 2 * HD, 4 * HD), BF16),
            pltpu.VMEM((HEADS, 2 * HD, 2 * TOK), BF16),
            pltpu.VMEM((HEADS, HD, TOK), BF16),
            pltpu.VMEM((HEADS, TOK, TOK), F32),
            pltpu.VMEM((HEADS, TOK, TOK), F32),
            pltpu.VMEM((TOK, half), BF16),
            pltpu.VMEM((2 * NB, TOK, half // NB), F32),
            pltpu.VMEM((NB, TOK, half // NB), F32),
            pltpu.VMEM((TOK, TOK), F32),
            pltpu.VMEM((40, HD), F32),
            pltpu.VMEM((TOK, HD), F32),
            pltpu.VMEM((1, TOK), F32),
            dma((6,)),
            dma((3,)), dma((st,)), dma((st,)),
            dma((3,)), dma((st,)), dma((st,)),
            dma((1,)), dma((NB,)),
            pltpu.SemaphoreType.REGULAR,
        ],
        compiler_params=pltpu.CompilerParams(collective_id=0, has_side_effects=True),
        name="mesa",
    )(
        query_rows, key_rows, value_rows,
        doc_lengths.reshape(1, -1), norm_gain.reshape(1, -1), out_weight,
    )


def solution(mesh):
    in_specs = (P("seq", "head"), P("seq", "head"), P("seq", "head"), P(), P(), P("head", None))
    return jax.shard_map(
        on_device, mesh=mesh, in_specs=in_specs, out_specs=P("seq", "head"), check_vma=False
    )
```

```python
import jax
import jax.numpy as jnp
from jax import lax
from jax.experimental import pallas as pl
from jax.experimental.pallas import tpu as pltpu
from jax.sharding import PartitionSpec as P

MESH = pl.DeviceIdType.MESH
F32 = jnp.float32
BF16 = jnp.bfloat16
HD = 128
TOK = 128
HEADS = 8
PAIRS = 4
ITERS = 4
CH = 64
CG = 40
CROSS = ((0, 1), (2, 3), (4, 5), (6,), (7,))
STAGES = PAIRS + len(CROSS)
LAST = 7
TURN = 4
NB = 4
epsilon = 1e-06
damping = 1.0

WR, WZ, WC, WP, WE, WEC = 0, 4, 8, 12, 16, 32


def split2(a):
    hi = a.astype(BF16)
    return hi, (a - hi.astype(F32)).astype(BF16)


def dot(a, b, dims):
    return lax.dot_general(a, b, (dims, ((), ())), preferred_element_type=F32)


NN, NT, TN = ((1,), (0,)), ((1,), (1,)), ((0,), (0,))


def kernel(
    q_hbm, k_hbm, v_hbm, len_hbm, gain_hbm, w_hbm, out_ref,
    q_ref, k_ref, v_ref, w_ref, len_ref, gain_ref,
    tbuf, ybuf, rbuf, zs, zr, eo, ebuf, qs, scq, lhs, xl, vt, mf, mg, nbuf, acc, other,
    mask_ref, wts, tail_ref, car_ref,
    lsem, sent, yr, xr, zsd, zrv, er, ps, pr, ready,
):
    s = lax.axis_index("seq")
    c = lax.axis_index("head")
    y = lax.rem(s, 4)
    row = s - y
    x = lax.rem(s // 4, 4)
    col = s - 4 * x
    z = s // 16

    def at_y(d):
        return row + lax.rem(y + d, 4)

    def at_x(d):
        return col + 4 * lax.rem(x + d, 4)

    barrier = pltpu.get_barrier_semaphore()
    for d in (1, 2, 3):
        pl.semaphore_signal(barrier, inc=1, device_id=(at_y(d), c), device_id_type=MESH)
        pl.semaphore_signal(barrier, inc=1, device_id=(at_x(d), c), device_id_type=MESH)
    pl.semaphore_signal(barrier, inc=1, device_id=(s, 1 - c), device_id_type=MESH)

    @pl.when(z < TURN)
    def _():
        pl.semaphore_signal(
            barrier, inc=1, device_id=(lax.rem(s + 16, 128), c), device_id_type=MESH
        )

    @pl.when(z > TURN)
    def _():
        pl.semaphore_signal(
            barrier, inc=1, device_id=(lax.rem(s + 112, 128), c), device_id_type=MESH
        )

    loads = [
        pltpu.make_async_copy(a, b, lsem.at[i])
        for i, (a, b) in enumerate(
            [
                (len_hbm, len_ref), (k_hbm, k_ref), (v_hbm, v_ref),
                (q_hbm, q_ref), (gain_hbm, gain_ref), (w_hbm, w_ref),
            ]
        )
    ]
    LEN, KEY, VAL, QUERY, GAIN, WEIGHT = loads
    for cp in loads:
        cp.start()

    @pl.when(z == 0)
    def _():
        zr[...] = jnp.zeros_like(zr)

    LEN.wait()
    lrow = len_ref[...].astype(F32)
    ri = lax.broadcasted_iota(jnp.int32, (TOK, TOK), 0)
    ci = lax.broadcasted_iota(jnp.int32, (TOK, TOK), 1)
    lcol = jnp.sum(jnp.where(ri == ci, lrow, 0.0), axis=1, keepdims=True)
    srow = jnp.sum(jnp.where(ri < ci, lcol, 0.0), axis=0, keepdims=True)
    scol = jnp.sum(jnp.where(ci < ri, lrow, 0.0), axis=1, keepdims=True)
    base = (s * TOK).astype(F32)
    rf, cf = ri.astype(F32), ci.astype(F32)
    doc_col = jnp.sum(jnp.where(srow <= base + rf, 1.0, 0.0), axis=1, keepdims=True)
    doc_row = jnp.sum(jnp.where(scol <= base + cf, 1.0, 0.0), axis=0, keepdims=True)
    ends = jnp.sum(jnp.where(scol <= cf * TOK + (TOK - 1.0), 1.0, 0.0), axis=0, keepdims=True)
    shard = lax.broadcasted_iota(jnp.int32, (1, TOK), 1)

    def end_of(i):
        return jnp.sum(jnp.where(shard == i, ends, 0.0), axis=1, keepdims=True)

    def put(k, flag):
        wts[k : k + 1, :] = jnp.broadcast_to(jnp.where(flag, 1.0, 0.0), (1, HD))

    here, before = end_of(s), end_of(s - 1)
    car_ref[...] = jnp.where(doc_row == before, 1.0, 0.0)
    tail_ref[...] = jnp.broadcast_to(jnp.where(doc_col == here, 1.0, 0.0), (TOK, HD))
    mask_ref[...] = jnp.where((doc_col == doc_row) & (ri <= ci), 1.0, 0.0)
    dy = [end_of(row + i) for i in range(4)]
    dx = [end_of(16 * z + 4 * i + 3) for i in range(4)]
    dprev, dplane = end_of(row - 1), end_of(16 * z - 1)
    for i in range(4):
        put(WR + i, dy[i] == dy[3])
        put(WZ + i, dx[i] == dx[3])
        put(WC + i, (dx[i] == dprev) & (jnp.full((1, 1), i, jnp.int32) < x))
    put(WP, (dplane == dprev) & (dplane > 0.0))
    for t in range(1, 4):
        for i in range(t):
            put(WE + 4 * t + i, dy[i] == dy[t - 1])
        put(WEC + t, dprev == dy[t - 1])

    def wt(k):
        return wts[k : k + 1, :]

    def head_cols(h):
        return pl.ds(pl.multiple_of(h * HD, HD), HD)

    def rows(st):
        return pl.ds(0, CG if st < PAIRS else 32 * len(CROSS[st - PAIRS]))

    def kind(st):
        return 0 if st < PAIRS else 1 if len(CROSS[st - PAIRS]) == 2 else 2

    def ycopy(st, d):
        r = rows(st)
        return pltpu.make_async_remote_copy(
            tbuf.at[st, lax.rem(y + d, 4), r], ybuf.at[st, y, r], sent.at[kind(st)], yr.at[st],
            device_id=(at_y(d), c), device_id_type=MESH,
        )

    def xcopy(st, d):
        r = rows(st)
        return pltpu.make_async_remote_copy(
            rbuf.at[st, x, r], rbuf.at[st, x, r], sent.at[kind(st)], xr.at[st],
            device_id=(at_x(d), c), device_id_type=MESH,
        )

    def zcopy(st):
        r = rows(st)
        return pltpu.make_async_remote_copy(
            zs.at[st, r], zr.at[st, r], zsd.at[kind(st)], zrv.at[st],
            device_id=(lax.rem(s + 16, 128), c), device_id_type=MESH,
        )

    def ecopy(st, d):
        r = rows(st)
        return pltpu.make_async_remote_copy(
            eo.at[st, lax.rem(y + d, 4), r], ebuf.at[st, y, r], sent.at[kind(st)], er.at[st],
            device_id=(at_y(d), c), device_id_type=MESH,
        )

    def wait_bytes(ref, sem):
        pltpu.make_async_copy(ref, ref, sem).wait()

    def arrived(ref, sem, st):
        wait_bytes(ref.at[st, pl.ds(0, 3), rows(st)], sem.at[st])

    def send_tail(st):
        r = rows(st)
        for d in (2, 1, 3):
            ycopy(st, d).start()
        ybuf[st, y, r] = tbuf[st, y, r]

    lane = lax.broadcasted_iota(jnp.int32, (32, HD), 1)

    def gram_stage(g):
        grams = []
        for h in (2 * g, 2 * g + 1):
            k = k_ref[:, head_cols(h)]
            kf = k.astype(F32)
            ks = lax.rsqrt(jnp.sum(kf * kf, axis=1, keepdims=True) + epsilon)
            hi, lo = split2(kf * (ks * ks) * tail_ref[...])
            grams.append(dot(jnp.concatenate([hi, lo], 0), jnp.concatenate([k, k], 0), TN))
        blocks = []
        for gram in grams:
            blocks.append(gram[:32])
            blocks.append(jnp.where(lane < 32, pltpu.roll(gram[96:], 32, 1), gram[32:64]))
        blocks.append(jnp.where(lane < 64, pltpu.roll(grams[1][64:96], 64, 1), grams[0][64:96]))
        packed = jnp.concatenate(blocks, 0)
        for o in range(4):
            tbuf[g, o, :CG] = packed[CG * o : CG * (o + 1)]

    def gram_of(g, i):
        packed = jnp.concatenate([ebuf[g, o, :CG] for o in range(4)], 0)
        first, second, third = packed[64 * i : 64 * i + 32], packed[64 * i + 32 : 64 * i + 64], packed[128:]
        if i == 1:
            third = pltpu.roll(third, 64, 1)
        upper = jnp.concatenate([first, second, third, pltpu.roll(second, 96, 1)], 0)
        return jnp.where(ci // 32 >= ri // 32, upper, upper.T)

    def cross_stage(st):
        parts = []
        for h in CROSS[st - PAIRS]:
            k = k_ref[:, head_cols(h)]
            v = v_ref[:, head_cols(h)]
            kf = k.astype(F32)
            ks = lax.rsqrt(jnp.sum(kf * kf, axis=1, keepdims=True) + epsilon)
            hi, lo = split2(kf * ks * tail_ref[...])
            parts.append(dot(jnp.concatenate([v, v], 0), jnp.concatenate([hi, lo], 0), TN))
        n = 32 * len(parts)
        stacked = jnp.concatenate(parts, 0)
        for o in range(4):
            tbuf[st, o, :n] = stacked[n * o : n * (o + 1)]

    def row_sum(st):
        r = rows(st)
        arrived(ybuf, yr, st)
        total = ybuf[st, 3, r]
        for i in range(3):
            total = total + wt(WR + i) * ybuf[st, i, r]
        rbuf[st, x, r] = total
        for d in (2, 1, 3):
            xcopy(st, d).start()

    def plane_sum(st):
        r = rows(st)
        arrived(rbuf, xr, st)
        total = rbuf[st, 3, r]
        for i in range(3):
            total = total + wt(WZ + i) * rbuf[st, i, r]
        zs[st, r] = total

        if st == 0:

            @pl.when(z < TURN)
            def _():
                pl.semaphore_wait(ready, 1)

        @pl.when(z < LAST)
        def _():
            zcopy(st).start()

    def give_back(st):
        r = rows(st)

        @pl.when(z > 0)
        def _():
            zcopy(st).wait_recv()

        come = wt(WP) * zr[st, r]
        for i in range(3):
            come = come + wt(WC + i) * rbuf[st, i, r]
        eo[st, 0, r] = come
        parts = [ybuf[st, i, r] for i in range(3)]
        for t in range(1, 4):
            total = wt(WEC + t) * come
            for i in range(t):
                total = total + wt(WE + 4 * t + i) * parts[i]
            eo[st, t, r] = total
        for d in (2, 1, 3):
            ecopy(st, d).start()
        ebuf[st, y, r] = eo[st, y, r]

    def prepare(g):
        for h in (2 * g, 2 * g + 1):
            q = q_ref[:, head_cols(h)].astype(F32).T
            q = q * lax.rsqrt(jnp.sum(q * q, axis=0, keepdims=True) + epsilon)
            k = k_ref[:, head_cols(h)]
            kf = k.astype(F32)
            ks = lax.rsqrt(jnp.sum(kf * kf, axis=1, keepdims=True) + epsilon)
            m = mask_ref[...] * ks
            mf[h] = m
            mg[h] = m * ks
            hi, lo = split2(q)
            qs[h] = q
            scq[h] = dot(jnp.concatenate([k, k], 1), jnp.concatenate([hi, lo], 0), NN)
            khi, klo = split2(dot(k, k, NT))
            lhs[h, :HD, HD : 2 * HD] = kf.T.astype(BF16)
            lhs[h, HD:, HD : 2 * HD] = khi
            lhs[h, :HD, 3 * HD :] = jnp.zeros_like(klo)
            lhs[h, HD:, 3 * HD :] = klo
            vt[h] = v_ref[:, head_cols(h)].astype(F32).T.astype(BF16)

    def columns_of(vector, scores):
        hi, lo = split2(vector)
        shi, slo = split2(scores)
        car16 = car_ref[...].astype(BF16)
        return jnp.concatenate([hi * car16, shi], 0), jnp.concatenate([lo * car16, slo], 0)

    def solve(pairs):
        state = []
        for g, i in [(g, i) for g in pairs for i in range(2)]:
            if i == 0:
                arrived(ebuf, er, g)
            h = 2 * g + i
            k = k_ref[:, head_cols(h)]
            ghi, glo = split2(gram_of(g, i))
            shi, slo = split2(dot(jnp.concatenate([k, k], 1), jnp.concatenate([ghi, glo], 0), NN))
            lhs[h, :HD, :HD] = ghi
            lhs[h, HD:, :HD] = shi
            lhs[h, :HD, 2 * HD : 3 * HD] = glo
            lhs[h, HD:, 2 * HD : 3 * HD] = slo
            q, sc = qs[h], scq[h]
            n = jnp.sum(q * q, axis=0, keepdims=True)
            state.append(dict(h=h, p=q, sp=sc, r=q, sr=sc, n=n))
            if i == 1:
                yield
        for it in range(ITERS):
            last = it == ITERS - 1
            rows_here = HD if last else 2 * HD
            for e in state:
                p, sp, h = e["p"], e["sp"], e["h"]
                hi, lo = columns_of(p, sp * mg[h])
                both = dot(lhs[h, :rows_here, : 2 * HD], jnp.concatenate([hi, lo], 1), NN)
                both = both[:, :TOK] + both[:, TOK:] + dot(lhs[h, :rows_here, 2 * HD :], hi, NN)
                a = both[:HD] + damping * p
                alpha = e["n"] / (jnp.sum(p * a, axis=0, keepdims=True) + epsilon)
                e["x"] = alpha * p if it == 0 else e["x"] + alpha * p
                e["sx"] = alpha * sp if it == 0 else e["sx"] + alpha * sp
                if not last:
                    sa = both[HD:] + damping * sp
                    e["r"] = e["r"] - alpha * a
                    e["sr"] = e["sr"] - alpha * sa
                    new = jnp.sum(e["r"] * e["r"], axis=0, keepdims=True)
                    beta = new / (e["n"] + epsilon)
                    e["p"] = e["r"] + beta * p
                    e["sp"] = e["sr"] + beta * sp
                    e["n"] = new
            yield
        for e in state:
            h = e["h"]
            hi, lo = columns_of(e["x"], e["sx"] * mf[h])
            xl[h] = jnp.concatenate([hi, lo], 1)

    def finish(*stages):
        for st in stages:
            arrived(ebuf, er, st)
        states = []
        for st in stages:
            n = 32 * len(CROSS[st - PAIRS])
            stacked = jnp.concatenate([ebuf[st, o, :n] for o in range(4)], 0)
            for i, h in enumerate(CROSS[st - PAIRS]):
                states.append((h, stacked[HD * i : HD * (i + 1)]))
        for h, cross in states:
            xhi, xlo = split2(cross)
            mixed = dot(jnp.concatenate([xhi, vt[h]], 1), xl[h], NN)
            mixed = mixed[:, :TOK] + mixed[:, TOK:] + dot(xlo, xl[h, :HD, :TOK], NN)
            inv = lax.rsqrt(jnp.sum(mixed * mixed, axis=0, keepdims=True) / HD + epsilon)
            nbuf[:, head_cols(h)] = (mixed * inv * gain_col()).T.astype(BF16)

    def gain_col():
        return jnp.sum(jnp.where(ri == ci, gain_ref[...], 0.0), axis=1, keepdims=True)

    half = HEADS * HD
    width = half // NB

    def columns(b):
        side = 1 - c if b < NB else c
        return pl.ds(pl.multiple_of(side * half + (b % NB) * width, width), width)

    def project(g, b):
        mine = slice(2 * HD * g, 2 * HD * (g + 1))
        return dot(nbuf[:, mine], w_ref[mine, columns(b)], NN)

    def project_pair(g):
        for b in range(2 * NB):
            acc[b] = project(g, b) if g == 0 else acc[b] + project(g, b)

    KEY.wait()
    gram_stage(0)
    greeted = jnp.where((z > 0) & (z <= TURN), 1, 0) + jnp.where((z >= TURN) & (z < LAST), 1, 0)
    pl.semaphore_wait(barrier, 7 + greeted)

    @pl.when((z > 0) & (z <= TURN))
    def _():
        pl.semaphore_signal(
            ready, inc=1, device_id=(lax.rem(s + 112, 128), c), device_id_type=MESH
        )

    def send_early(st):
        @pl.when(c == 0)
        def _():
            send_tail(st)

    def send_late(st):
        @pl.when(c == 1)
        def _():
            send_tail(st)

    send_tail(0)
    for g in range(1, PAIRS):
        gram_stage(g)
        send_early(g)
        if g > 1:
            send_late(g - 1)
    VAL.wait()
    for st in range(PAIRS, STAGES):
        cross_stage(st)
        send_early(st)
        if st == PAIRS:
            send_late(PAIRS - 1)
    row_sum(0)
    row_sum(1)
    send_late(4)
    QUERY.wait()
    prepare(0)
    row_sum(2)
    send_late(5)
    row_sum(3)
    send_late(6)
    prepare(1)
    send_late(7)
    send_late(8)
    row_sum(4)
    plane_sum(0)
    plane_sum(1)
    row_sum(5)
    plane_sum(2)
    give_back(0)
    plane_sum(3)
    row_sum(6)
    give_back(1)
    prepare(2)
    row_sum(7)
    row_sum(8)
    plane_sum(4)
    give_back(2)
    prepare(3)
    plane_sum(5)
    give_back(3)
    first = solve((0, 1))
    next(first)
    plane_sum(6)
    give_back(4)
    next(first)
    next(first)
    give_back(5)
    plane_sum(7)
    plane_sum(8)
    next(first)
    next(first)
    give_back(6)
    for _ in first:
        pass
    second = solve((2, 3))
    next(second)
    next(second)
    give_back(7)
    give_back(8)
    for _ in second:
        pass
    GAIN.wait()
    WEIGHT.wait()
    finish(4, 5)
    project_pair(0)
    project_pair(1)
    finish(6)
    project_pair(2)
    finish(7, 8)

    def pcopy(b):
        return pltpu.make_async_remote_copy(
            acc.at[b], other.at[b], ps.at[0], pr.at[b],
            device_id=(s, 1 - c), device_id_type=MESH,
        )

    for b in range(0, NB, 2):
        for e in (b, b + 1):
            acc[e] = acc[e] + project(PAIRS - 1, e)
        for e in (b, b + 1):
            pcopy(e).start()
    for b in range(NB, 2 * NB):
        acc[b] = acc[b] + project(PAIRS - 1, b)
    for b in range(NB):
        pcopy(b).wait_recv()
        out_ref[:, b * width : (b + 1) * width] = (acc[NB + b] + other[b]).astype(BF16)

    for i, (stages, slots) in enumerate(((9, 4), (9, 3), (6, 3))):
        group = [st for st in range(STAGES) if kind(st) == i]
        wait_bytes(ybuf.at[pl.ds(0, stages), pl.ds(0, slots), rows(group[0])], sent.at[i])

        @pl.when(z < LAST)
        def _():
            wait_bytes(zs.at[pl.ds(group[0], len(group)), rows(group[0])], zsd.at[i])

    wait_bytes(other, ps.at[0])


def on_device(query_rows, key_rows, value_rows, doc_lengths, norm_gain, out_weight):
    half = HEADS * HD
    st = STAGES
    dma = pltpu.SemaphoreType.DMA
    anywhere = pl.BlockSpec(memory_space=pl.ANY)
    return pl.pallas_call(
        kernel,
        out_shape=pltpu.VMEM((TOK, half), BF16),
        in_specs=[anywhere] * 6,
        out_specs=pl.BlockSpec(memory_space=pltpu.VMEM),
        scratch_shapes=[
            pltpu.VMEM((TOK, half), BF16),
            pltpu.VMEM((TOK, half), BF16),
            pltpu.VMEM((TOK, half), BF16),
            pltpu.VMEM((half, 2 * half), BF16),
            pltpu.VMEM((1, HD), jnp.int32),
            pltpu.VMEM((1, HD), F32),
            pltpu.VMEM((st, 4, CH, HD), F32),
            pltpu.VMEM((st, 4, CH, HD), F32),
            pltpu.VMEM((st, 4, CH, HD), F32),
            pltpu.VMEM((st, CH, HD), F32),
            pltpu.VMEM((st, CH, HD), F32),
            pltpu.VMEM((st, 4, CH, HD), F32),
            pltpu.VMEM((st, 4, CH, HD), F32),
            pltpu.VMEM((HEADS, TOK, HD), F32),
            pltpu.VMEM((HEADS, TOK, TOK), F32),
            pltpu.VMEM((HEADS, 2 * HD, 4 * HD), BF16),
            pltpu.VMEM((HEADS, 2 * HD, 2 * TOK), BF16),
            pltpu.VMEM((HEADS, HD, TOK), BF16),
            pltpu.VMEM((HEADS, TOK, TOK), F32),
            pltpu.VMEM((HEADS, TOK, TOK), F32),
            pltpu.VMEM((TOK, half), BF16),
            pltpu.VMEM((2 * NB, TOK, half // NB), F32),
            pltpu.VMEM((NB, TOK, half // NB), F32),
            pltpu.VMEM((TOK, TOK), F32),
            pltpu.VMEM((40, HD), F32),
            pltpu.VMEM((TOK, HD), F32),
            pltpu.VMEM((1, TOK), F32),
            dma((6,)),
            dma((3,)), dma((st,)), dma((st,)),
            dma((3,)), dma((st,)), dma((st,)),
            dma((1,)), dma((NB,)),
            pltpu.SemaphoreType.REGULAR,
        ],
        compiler_params=pltpu.CompilerParams(collective_id=0, has_side_effects=True),
        name="mesa",
    )(
        query_rows, key_rows, value_rows,
        doc_lengths.reshape(1, -1), norm_gain.reshape(1, -1), out_weight,
    )


def solution(mesh):
    in_specs = (P("seq", "head"), P("seq", "head"), P("seq", "head"), P(), P(), P("head", None))
    return jax.shard_map(
        on_device, mesh=mesh, in_specs=in_specs, out_specs=P("seq", "head"), check_vma=False
    )
```
